256 devices in a mesh: row: 8 (over x_lo, y), col: 32 (over z, x_hi, core).
Axes of the slice: x: 4 (x_hi: 2, x_lo: 2; x = x_hi * 2 + x_lo), y: 4, z: 8, core: 2. Of those that a mesh axis runs over, the one named last changes fastest.
Arguments:
- b_steps: float32 [2, 1024, 8192], P(None, 'row', 'col'), may hold values from -6 to 6
- b_trail: float32 [8192, 8192], P('row', 'col'), may hold values from -6 to 6
- l_cross: float32 [1024, 1024], P('row', 'col'), may hold values from -0.1875 to 0.1875
- l_trail: float32 [2, 8192, 1024], P(None, 'row', 'col'), may hold values from -0.125 to 0.125
- diag_inv: float32 [2, 2, 512, 512], P(None, None, None, 'col'), may hold values from -1.5 to 1.5, as said below
- diag_low: float32 [2, 512, 512], P(None, None, 'col'), may hold values from -0.25 to 0.25
Outputs:
- x_steps: float32 [2, 1024, 8192], P(None, 'row', 'col')
- trail_out: float32 [8192, 8192], P('row', 'col')
The draws below stay inside these ranges and needn't reach their ends.
Inputs may be any that keep to these rules, and one draw needn't show every extreme that they name: Each diag_inv[s, h] is lower triangular with diagonal entries of 0.5 to 1.5 and strictly lower entries of magnitude at most 3 / sqrt(512).
All inputs are finite; a program needn't handle non-finite values.
Results may differ from the reference program's by a relative error of at most 0.00013.
Values sent between devices are 32-bit elements; how exact they have to be, the bound alone decides.
A program may use at most 64 MiB of HBM per device.

```python
import math
import jax
import jax.numpy as jnp
from jax import lax

NB = 1024
H = 512
RHS = 8192
TRAIL = 8192


def draw_diag_inv(key, part):
    key_strict = jax.random.fold_in(key, 11)
    key_diagonal = jax.random.fold_in(key, 23)
    array_dims = (2, 2, H, H)
    strict = jnp.clip(jax.random.normal(key_strict, array_dims, jnp.float32), -3.0, 3.0) / math.sqrt(H)
    diagonal = jax.random.uniform(key_diagonal, (2, 2, H), jnp.float32, 0.5, 1.5)
    lower = jnp.tril(strict, -1) + diagonal[..., None] * jnp.eye(H, dtype=jnp.float32)
    return lower.astype(jnp.float32)


def levels(key, shape, split, least, largest):
    def one(axis_at, parts):
        draws = jax.random.uniform(jax.random.fold_in(jax.random.fold_in(key, 6), axis_at), (parts,), jnp.float32, least / len(split), largest / len(split))
        return jnp.repeat(jnp.exp(draws), shape[axis_at] // parts).reshape((-1,) + (1,) * (len(shape) - axis_at - 1))

    loudness = one(*split[0])
    for cut in split[1:]:
        loudness = loudness * one(*cut)
    return loudness


def normal_values(rng, extent, scale, limit, shards=(), kind=jnp.bfloat16):
    array = scale * jax.random.normal(rng, extent, jnp.float32)
    if shards:
        array = array * levels(rng, extent, shards, -0.22, 0.18)
    return jnp.clip(array, -limit, limit).astype(kind)


def setup_inputs(seed: int = 0) -> dict:
    splits = jax.random.split(jax.random.key(seed), 7)
    return {
        "b_steps": normal_values(splits[0], (2, NB, RHS), 1.0, 6.0, ((1, 8), (2, 32)), jnp.float32),
        "b_trail": normal_values(splits[1], (TRAIL, RHS), 1.0, 6.0, ((0, 8), (1, 32)), jnp.float32),
        "l_cross": normal_values(splits[2], (NB, NB), NB ** -0.5, 0.1875, ((0, 8), (1, 32)), jnp.float32),
        "l_trail": normal_values(splits[3], (2, TRAIL, NB), (2 * NB) ** -0.5, 0.125, ((1, 8), (2, 32)), jnp.float32),
        "diag_inv": draw_diag_inv(jax.random.fold_in(splits[6], 71), 0),
        "diag_low": normal_values(splits[5], (2, H, H), H ** -0.5, 0.25, ((2, 32),), jnp.float32),
    }


exact_prec = lax.Precision.HIGHEST


def mult(left_mat, right_mat):
    return jnp.dot(left_mat, right_mat, precision=exact_prec, preferred_element_type=jnp.float32)


def joined_inverse(inv_pair, low_block):
    inv_first = inv_pair[0]
    inv_second = inv_pair[1]
    lower_left = -mult(inv_second, mult(low_block, inv_first))
    upper = jnp.concatenate([inv_first, jnp.zeros_like(inv_first)], 1)
    bottom = jnp.concatenate([lower_left, inv_second], 1)
    return jnp.concatenate([upper, bottom], 0)


def reference(b_steps, b_trail, l_cross, l_trail, diag_inv, diag_low):
    joined_first = joined_inverse(diag_inv[0], diag_low[0])
    solved_first = mult(joined_first, b_steps[0])
    next_rows = b_steps[1] - mult(l_cross, solved_first)
    trail_mid = b_trail - mult(l_trail[0], solved_first)
    joined_second = joined_inverse(diag_inv[1], diag_low[1])
    solved_second = mult(joined_second, next_rows)
    trail_out = trail_mid - mult(l_trail[1], solved_second)
    return jnp.stack([solved_first, solved_second]), trail_out
```

```python
import jax
import jax.numpy as jnp
from jax import lax
from jax.experimental import pallas as pl
from jax.experimental.pallas import tpu as pltpu
from jax.sharding import PartitionSpec as P

MESH = pl.DeviceIdType.MESH
F32 = jnp.float32
BF16 = jnp.bfloat16

NY, NZ = 4, 8
RING = (0, 1, 7, 2, 6, 3, 5, 4)
N_SEM = 256


def split(value):
    high = value.astype(BF16)
    return high, (value - high.astype(F32)).astype(BF16)


def product(left, right):
    dot = lambda a, b: jnp.dot(a, b, preferred_element_type=F32)
    return dot(left[0], right[0]) + (dot(left[0], right[1]) + dot(left[1], right[0]))


def kernel(
    b_steps, b_trail, cross, trail, inv, low,
    x_out, t_out,
    lf, tab, crs, rhs, xs, acc, bs, bt, xo, to,
    ss, rs, ls, os,
):
    row, col = lax.axis_index("row"), lax.axis_index("col")
    xl, y = row // NY, row % NY
    z, xh, k = col // 4, (col // 2) % 2, col % 2

    def dev(dxl=0, dy=0, dz=0, dxh=0, dk=0):
        a = (1 - xl) if dxl else xl
        b = (1 - xh) if dxh else xh
        c = (1 - k) if dk else k
        return (a * NY + (y + dy) % NY, ((z + dz) % NZ) * 4 + b * 2 + c)

    ids = {}

    def sem(name):
        return ids.setdefault(name, len(ids))

    started = []

    def send(name, src, dst, to_dev):
        i = sem(name)
        copy = pltpu.make_async_remote_copy(
            src_ref=src, dst_ref=dst, send_sem=ss.at[i], recv_sem=rs.at[i],
            device_id=to_dev, device_id_type=MESH)
        copy.start()
        started.append(copy)

    def recv(name, region, from_dev):
        i = sem(name)
        pltpu.make_async_remote_copy(
            src_ref=region, dst_ref=region, send_sem=ss.at[i], recv_sem=rs.at[i],
            device_id=from_dev, device_id_type=MESH).wait_recv()

    partners = [dev(dz=e) for e in range(1, NZ)] + [dev(dy=1), dev(dy=3), dev(dxl=1), dev(dxh=1), dev(dk=1)]
    barrier = pltpu.get_barrier_semaphore()
    for p in partners:
        pl.semaphore_signal(barrier, inc=1, device_id=p, device_id_type=MESH)
    loads = []

    def load(src, dst):
        copy = pltpu.make_async_copy(src, dst, ls.at[len(loads)])
        copy.start()
        loads.append(copy)

    lanes = pl.ds(pl.multiple_of(y * 128, 128), 128)
    load(b_steps, bs)
    load(cross, crs.at[z, k, xh])
    for s in range(2):
        mine = tab.at[s, z, k, y, xh]
        load(inv.at[s, 0, :, lanes], mine.at[pl.ds(0, 16)])
        load(low.at[s, :, lanes], mine.at[pl.ds(16, 16)])
        load(inv.at[s, 1, :, lanes], mine.at[pl.ds(32, 16)])
    for s in range(2):
        load(trail.at[s], lf.at[s, z, k, xh])
    load(b_trail, bt)
    for c in loads[:8]:
        c.wait()
    pl.semaphore_wait(barrier, len(partners))

    def zrel(e):
        return (z + NZ - e) % NZ

    def t_zsend(g):
        for e in range(1, NZ):
            blk = tab.at[g, z, k, y, xh]
            send(("tz", g, e), blk, blk, dev(dz=e))
            if g == 0:
                blk = crs.at[z, k, xh]
                send(("cz", e), blk, blk, dev(dz=e))

    def t_xsend(g, e):
        blk = tab.at[g, zrel(e), k, y, xh]
        if e:
            recv(("tz", g, e), blk, dev(dz=NZ - e))
        send(("tx", g, e), blk, blk, dev(dxh=1))
        if g == 0:
            blk = crs.at[zrel(e), k, xh]
            if e:
                recv(("cz", e), blk, dev(dz=NZ - e))
            send(("cx", e), blk, blk, dev(dxh=1))

    def t_ysend(g, e):
        recv(("tx", g, e), tab.at[g, zrel(e), k, y, 1 - xh], dev(dxh=1))
        blk = tab.at[g, zrel(e), k, y]
        send(("ty+", g, e), blk, blk, dev(dy=1))
        send(("ty-", g, e), blk, blk, dev(dy=3))

    def t_yforward(g, e):
        recv(("ty+", g, e), tab.at[g, zrel(e), k, (y + 3) % NY], dev(dy=3))
        blk = tab.at[g, zrel(e), k, (y + 3) % NY, 0]
        send(("tf+", g, e), blk, blk, dev(dy=1))
        recv(("ty-", g, e), tab.at[g, zrel(e), k, (y + 1) % NY], dev(dy=1))
        blk = tab.at[g, zrel(e), k, (y + 1) % NY, 1]
        send(("tf-", g, e), blk, blk, dev(dy=3))

    def t_core(g, e):
        far = (y + 2) % NY
        recv(("tf+", g, e), tab.at[g, zrel(e), k, far, 0], dev(dy=3))
        recv(("tf-", g, e), tab.at[g, zrel(e), k, far, 1], dev(dy=1))
        blk = tab.at[g, zrel(e), k]
        send(("tk", g, e), blk, blk, dev(dk=1))
        if g == 0:
            recv(("cx", e), crs.at[zrel(e), k, 1 - xh], dev(dxh=1))
            blk = crs.at[zrel(e), k]
            send(("ck", e), blk, blk, dev(dk=1))

    def t_done(g, e):
        recv(("tk", g, e), tab.at[g, zrel(e), 1 - k], dev(dk=1))
        if g == 0:
            recv(("ck", e), crs.at[zrel(e), 1 - k], dev(dk=1))

    def l_hop(s, h):
        for sign, last in ((1, 4 if s == 0 else 3), (-1, 3 if s == 0 else 4)):
            if h > last:
                continue
            at = zrel(h if sign > 0 else NZ - h)
            blk = lf.at[s, at, k] if s == 0 else lf.at[s, at, k, xh]
            if h:
                recv(("l", s, sign, h), blk, dev(dz=NZ - sign))
            if h < last:
                send(("l", s, sign, h + 1), blk, blk, dev(dz=sign % NZ))
            if h == 0 and sign < 0:
                continue
            if s == 0:
                send(("lk", s, sign * h), blk, blk, dev(dk=1))
            else:
                send(("lx", s, sign * h), blk, blk, dev(dxh=1))

    def l_cross(s, h):
        for sign, last in ((1, 3), (-1, 4)):
            if h > last or (h == 0 and sign < 0):
                continue
            at = zrel(h if sign > 0 else NZ - h)
            recv(("lx", s, sign * h), lf.at[s, at, k, 1 - xh], dev(dxh=1))
            blk = lf.at[s, at, k]
            send(("lk", s, sign * h), blk, blk, dev(dk=1))

    def l_done(s, h):
        for sign, last in ((1, 4 if s == 0 else 3), (-1, 3 if s == 0 else 4)):
            if h > last or (h == 0 and sign < 0):
                continue
            at = zrel(h if sign > 0 else NZ - h)
            recv(("lk", s, sign * h), lf.at[s, at, 1 - k], dev(dk=1))

    def r_send(g):
        blk = rhs.at[g, xl, y]
        send(("rx", g), blk, blk, dev(dxl=1))
        send(("ry+", g, 0), blk, blk, dev(dy=1))
        send(("ry-", g, 0), blk, blk, dev(dy=3))

    def r_other(g):
        blk = rhs.at[g, 1 - xl, y]
        recv(("rx", g), blk, dev(dxl=1))
        send(("ry+", g, 1), blk, blk, dev(dy=1))
        send(("ry-", g, 1), blk, blk, dev(dy=3))

    def r_forward(g):
        for j in range(2):
            which = xl if j == 0 else 1 - xl
            recv(("ry+", g, j), rhs.at[g, which, (y + 3) % NY], dev(dy=3))
            recv(("ry-", g, j), rhs.at[g, which, (y + 1) % NY], dev(dy=1))
            if j == 0:
                blk = rhs.at[g, which, (y + 3) % NY]
                send(("rf", g, j), blk, blk, dev(dy=1))
            else:
                blk = rhs.at[g, which, (y + 1) % NY]
                send(("rf", g, j), blk, blk, dev(dy=3))

    def r_done(g):
        far = (y + 2) % NY
        recv(("rf", g, 0), rhs.at[g, xl, far], dev(dy=3))
        recv(("rf", g, 1), rhs.at[g, 1 - xl, far], dev(dy=1))

    places = [(a, c, b) for a in range(NZ) for b in range(2) for c in range(2)]

    def weights(s, which, pair):
        halves = [
            jnp.concatenate([tab[s, a, c, 2 * pair + j, b, 16 * which:16 * which + 16, :] for a, c, b in places], axis=0)
            for j in range(2)
        ]
        return split(jnp.concatenate(halves, axis=1))

    def solve(s):
        top = split(jnp.concatenate([rhs[s, 0, j] for j in range(4)], axis=1))
        for pair in range(2):
            out = product(top, weights(s, 0, pair))
            xs[s, 2 * pair] = out[:, :128]
            xs[s, 2 * pair + 1] = out[:, 128:]
        first = split(jnp.concatenate([xs[s, j] for j in range(4)], axis=1))
        rest = []
        for pair in range(2):
            out = product(first, weights(s, 1, pair))
            rest.append(rhs[s, 1, 2 * pair] - out[:, :128])
            rest.append(rhs[s, 1, 2 * pair + 1] - out[:, 128:])
        rest = split(jnp.concatenate(rest, axis=1))
        for pair in range(2):
            out = product(rest, weights(s, 2, pair))
            xs[s, 4 + 2 * pair] = out[:, :128]
            xs[s, 5 + 2 * pair] = out[:, 128:]

    def whole(s):
        return split(jnp.concatenate([xs[s, j] for j in range(8)], axis=1))

    def emit(s):
        xo[s] = xs[s, row].T
        copy = pltpu.make_async_copy(xo.at[s], x_out.at[s], os.at[s])
        copy.start()
        return copy

    t_zsend(0)
    rhs[0, xl, y] = bs[0].T
    r_send(0)
    t_xsend(0, 0)
    for c in loads[8:10]:
        c.wait()
    own = lf.at[0, z, k, xh]
    send(("l0x",), own, own, dev(dxh=1))
    l_hop(1, 0)
    r_other(0)
    recv(("l0x",), lf.at[0, z, k, 1 - xh], dev(dxh=1))
    l_hop(0, 0)
    t_zsend(1)
    r_forward(0)
    for i in range(NZ + 4):
        if 0 < i < NZ:
            t_xsend(0, RING[i])
        if 0 <= i - 1 < NZ:
            t_ysend(0, RING[i - 1])
        if 0 <= i - 2 < NZ:
            t_yforward(0, RING[i - 2])
        if 0 <= i - 3 < NZ:
            t_core(0, RING[i - 3])
        if i == 4:
            l_hop(1, 1)
            l_cross(1, 0)
        if i == 6:
            l_hop(0, 1)
        if i == 9:
            l_hop(1, 2)
            l_cross(1, 1)
        if i == 11:
            l_hop(0, 2)
    r_done(0)
    for e in RING:
        t_done(0, e)
    solve(0)
    low_cross = split(jnp.concatenate([crs[a, c, b] for a, c, b in places], axis=0))
    rhs[1, xl, y] = bs[1].T - product(whole(0), low_cross)
    r_send(1)
    copies = [emit(0)]
    r_other(1)
    for i in range(NZ + 4):
        if i < NZ:
            t_xsend(1, RING[i])
        if 0 <= i - 1 < NZ:
            t_ysend(1, RING[i - 1])
        if 0 <= i - 2 < NZ:
            t_yforward(1, RING[i - 2])
        if 0 <= i - 3 < NZ:
            t_core(1, RING[i - 3])
        if i == 3:
            r_forward(1)
        if i == 6:
            l_hop(1, 3)
            l_cross(1, 2)
        if i == 9:
            l_hop(0, 3)
    r_done(1)
    l_hop(1, 4)
    l_cross(1, 3)
    l_hop(0, 4)
    l_cross(1, 4)
    for h in range(5):
        l_done(0, h)

    def tile(s, j):
        at = pl.ds(pl.multiple_of(j * 256, 256), 256)
        return split(jnp.concatenate([lf[s, a, c, b, :, at] for a, c, b in places], axis=0))

    first = whole(0)

    @pl.loop(0, 4)
    def _(j):
        acc[j] = product(first, tile(0, j))

    for e in RING:
        t_done(1, e)
    solve(1)
    copies.append(emit(1))
    for h in range(5):
        l_done(1, h)
    second = whole(1)
    loads[10].wait()

    @pl.loop(0, 4)
    def _(j):
        at = pl.ds(pl.multiple_of(j * 256, 256), 256)
        to[at, :] = bt[at, :] - (acc[j] + product(second, tile(1, j))).T

    last = pltpu.make_async_copy(to, t_out, os.at[2])
    last.start()
    for c in copies:
        c.wait()
    last.wait()
    for c in started:
        c.wait_send()
    assert len(ids) <= N_SEM


def shards(b_steps, b_trail, cross, trail, inv, low):
    anywhere = pl.BlockSpec(memory_space=pl.ANY)
    return pl.pallas_call(
        kernel,
        out_shape=(
            jax.ShapeDtypeStruct((2, 128, 256), F32),
            jax.ShapeDtypeStruct((1024, 256), F32),
        ),
        in_specs=[anywhere] * 6,
        out_specs=(anywhere, anywhere),
        scratch_shapes=[
            pltpu.VMEM((2, NZ, 2, 2, 32, 1024), F32),
            pltpu.VMEM((2, NZ, 2, NY, 2, 48, 128), F32),
            pltpu.VMEM((NZ, 2, 2, 32, 128), F32),
            pltpu.VMEM((2, 2, NY, 256, 128), F32),
            pltpu.VMEM((2, 8, 256, 128), F32),
            pltpu.VMEM((4, 256, 256), F32),
            pltpu.VMEM((2, 128, 256), F32),
            pltpu.VMEM((1024, 256), F32),
            pltpu.VMEM((2, 128, 256), F32),
            pltpu.VMEM((1024, 256), F32),
            pltpu.SemaphoreType.DMA((N_SEM,)),
            pltpu.SemaphoreType.DMA((N_SEM,)),
            pltpu.SemaphoreType.DMA((16,)),
            pltpu.SemaphoreType.DMA((4,)),
        ],
        compiler_params=pltpu.CompilerParams(
            collective_id=0, has_side_effects=True, vmem_limit_bytes=56 << 20),
    )(
        b_steps, b_trail, cross.T, jnp.swapaxes(trail, 1, 2),
        jnp.swapaxes(inv, 2, 3), jnp.swapaxes(low, 1, 2),
    )


def solution(mesh):
    placed = (
        P(None, "row", "col"),
        P("row", "col"),
        P("row", "col"),
        P(None, "row", "col"),
        P(None, None, None, "col"),
        P(None, None, "col"),
    )
    return jax.shard_map(
        shards,
        mesh=mesh,
        in_specs=placed,
        out_specs=(P(None, "row", "col"), P("row", "col")),
        check_vma=False,
    )
```

```python
import jax
import jax.numpy as jnp
from jax import lax
from jax.experimental import pallas as pl
from jax.experimental.pallas import tpu as pltpu
from jax.sharding import PartitionSpec as P

MESH = pl.DeviceIdType.MESH
F32 = jnp.float32
BF16 = jnp.bfloat16

NY, NZ = 4, 8
PAIRS = (0, 1, 3, 2)
N_SEND, N_RECV = 32, 128


def split(value):
    high = value.astype(BF16)
    return high, (value - high.astype(F32)).astype(BF16)


def product(left, right):
    dot = lambda a, b: jnp.dot(a, b, preferred_element_type=F32)
    return dot(left[0], right[0]) + (dot(left[0], right[1]) + dot(left[1], right[0]))


def kernel(
    b_steps, b_trail, cross, trail, inv, low,
    x_out, t_out,
    lf, tab, crs, rhs, xs, acc, bs, bt, xo, to,
    ss, rs, ls, os,
):
    row, col = lax.axis_index("row"), lax.axis_index("col")
    xl, y = row // NY, row % NY
    z, xh, k = col // 4, (col // 2) % 2, col % 2

    def dev(dxl=0, dy=0, dz=0, dxh=0, dk=0):
        a = (1 - xl) if dxl else xl
        b = (1 - xh) if dxh else xh
        c = (1 - k) if dk else k
        return (a * NY + (y + dy) % NY, ((z + dz) % NZ) * 4 + b * 2 + c)

    ids, streams = {}, {}

    def sem(name):
        return ids.setdefault(name, len(ids))

    def out_sem(stream):
        return streams.setdefault(stream, len(streams))

    def send(stream, at, src, dst, to_dev):
        pltpu.make_async_remote_copy(
            src_ref=src, dst_ref=dst, send_sem=ss.at[out_sem(stream)],
            recv_sem=rs.at[sem(stream) if at is None else sem((stream, at))],
            device_id=to_dev, device_id_type=MESH).start()

    def recv(stream, at, region, from_dev):
        i = sem(stream) if at is None else sem((stream, at)) if isinstance(at, tuple) else at
        pltpu.make_async_remote_copy(
            src_ref=region, dst_ref=region, send_sem=ss.at[out_sem(stream)], recv_sem=rs.at[i],
            device_id=from_dev, device_id_type=MESH).wait_recv()

    def sent(stream, region):
        pltpu.make_async_remote_copy(
            src_ref=region, dst_ref=region, send_sem=ss.at[streams[stream]], recv_sem=rs.at[0],
            device_id=dev(dk=1), device_id_type=MESH).wait_send()

    partners = [dev(dz=e) for e in range(1, NZ)] + [dev(dy=1), dev(dy=3), dev(dxl=1), dev(dxh=1), dev(dk=1)]
    barrier = pltpu.get_barrier_semaphore()
    for p in partners:
        pl.semaphore_signal(barrier, inc=1, device_id=p, device_id_type=MESH)
    loads = []

    def load(src, dst):
        copy = pltpu.make_async_copy(src, dst, ls.at[len(loads)])
        copy.start()
        loads.append(copy)

    lanes = pl.ds(pl.multiple_of(y * 128, 128), 128)
    load(b_steps, bs)
    load(cross, crs.at[k, xh, z])
    for s in range(2):
        mine = tab.at[s, k, z, y, xh]
        load(inv.at[s, 0, :, lanes], mine.at[pl.ds(0, 16)])
        load(low.at[s, :, lanes], mine.at[pl.ds(16, 16)])
        load(inv.at[s, 1, :, lanes], mine.at[pl.ds(32, 16)])
    for s in range(2):
        load(trail.at[s], lf.at[s, z, k, xh])
    load(b_trail, bt)
    for c in loads[:8]:
        c.wait()
    pl.semaphore_wait(barrier, len(partners))

    def pair(d):
        return (z // 2 + d) % (NZ // 2)

    tz = [[sem(("tz", g, e)) for e in range(NZ)] for g in range(2)]

    def t_zsend(g):
        blk = tab.at[g, k, z, y, xh]
        for e in range(1, NZ):
            pltpu.make_async_remote_copy(
                src_ref=blk, dst_ref=blk, send_sem=ss.at[out_sem(("tz", g))], recv_sem=rs.at[tz[g][e]],
                device_id=dev(dz=e), device_id_type=MESH).start()

    def t_x(g, d):
        zz = pair(d)
        for from_z in [2 * zz, 2 * zz + 1] if d else [z + 1 - 2 * (z % 2)]:
            e = (z - from_z + NZ) % NZ
            recv(("tz", g), tz[g][0] + e, tab.at[g, k, from_z, y, xh], dev(dz=1))
        blk = tab.at[g, k, pl.ds(2 * zz, 2), y, xh]
        send(("tx", g), (d,), blk, blk, dev(dxh=1))

    def t_y(g, d):
        zs = pl.ds(2 * pair(d), 2)
        recv(("tx", g), (d,), tab.at[g, k, zs, y, 1 - xh], dev(dxh=1))
        blk = tab.at[g, k, zs, y]
        send(("ty+", g), (d,), blk, blk, dev(dy=1))
        send(("ty-", g), (d,), blk, blk, dev(dy=3))

    def t_f(g, d):
        zs = pl.ds(2 * pair(d), 2)
        recv(("ty+", g), (d,), tab.at[g, k, zs, (y + 3) % NY], dev(dy=3))
        blk = tab.at[g, k, zs, (y + 3) % NY, 0]
        send(("tf+", g), (d,), blk, blk, dev(dy=1))
        recv(("ty-", g), (d,), tab.at[g, k, zs, (y + 1) % NY], dev(dy=1))
        blk = tab.at[g, k, zs, (y + 1) % NY, 1]
        send(("tf-", g), (d,), blk, blk, dev(dy=3))

    def t_k(g, d):
        zs = pl.ds(2 * pair(d), 2)
        far = (y + 2) % NY
        recv(("tf+", g), (d,), tab.at[g, k, zs, far, 0], dev(dy=3))
        recv(("tf-", g), (d,), tab.at[g, k, zs, far, 1], dev(dy=1))
        blk = tab.at[g, k, zs]
        send(("tk", g), None, blk, blk, dev(dk=1))

    def t_done(g):
        recv(("tk", g), None, tab.at[g, 1 - k], dev(dk=1))

    def t_sent(g):
        sent(("tz", g), tab.at[g, k, pl.ds(0, NZ - 1), y, xh])
        sent(("tx", g), tab.at[g, k, :, y, xh])
        for sign in "+-":
            sent(("ty" + sign, g), tab.at[g, k, :, y])
            sent(("tf" + sign, g), tab.at[g, k, :, y, xh])
        sent(("tk", g), tab.at[g, k])

    def c_z():
        blk = crs.at[k, xh, z]
        for e in range(1, NZ):
            send("cz", None, blk, blk, dev(dz=e))

    def c_x():
        recv("cz", None, crs.at[k, xh, pl.ds(0, NZ - 1)], dev(dz=1))
        send("cx", None, crs.at[k, xh], crs.at[k, xh], dev(dxh=1))

    def c_k():
        recv("cx", None, crs.at[k, 1 - xh], dev(dxh=1))
        send("ck", None, crs.at[k], crs.at[k], dev(dk=1))

    def c_done():
        recv("ck", None, crs.at[1 - k], dev(dk=1))

    def c_sent():
        sent("cz", crs.at[k, xh, pl.ds(0, NZ - 1)])
        sent("cx", crs.at[k, xh])
        sent("ck", crs.at[k])

    def zrel(e):
        return (z + NZ - e) % NZ

    def l_hop(s, h):
        for sign, last in ((1, 4 if s == 0 else 3), (-1, 3 if s == 0 else 4)):
            if h > last:
                continue
            at = zrel(h if sign > 0 else NZ - h)
            blk = lf.at[s, at, k] if s == 0 else lf.at[s, at, k, xh]
            if h:
                recv(("l", s), (sign, h), blk, dev(dz=NZ - sign))
            if h < last:
                send(("l", s), (sign, h + 1), blk, blk, dev(dz=sign % NZ))
            if h == 0 and sign < 0:
                continue
            if s == 0:
                send(("lk", s), None, blk, blk, dev(dk=1))
            else:
                send(("lx", s), (sign * h,), blk, blk, dev(dxh=1))

    def l_cross(s, h):
        for sign, last in ((1, 3), (-1, 4)):
            if h > last or (h == 0 and sign < 0):
                continue
            at = zrel(h if sign > 0 else NZ - h)
            recv(("lx", s), (sign * h,), lf.at[s, at, k, 1 - xh], dev(dxh=1))
            blk = lf.at[s, at, k]
            send(("lk", s), None, blk, blk, dev(dk=1))

    def l_done(s):
        recv(("lk", s), None, lf.at[s, :, 1 - k], dev(dk=1))

    def l_sent():
        sent("l0x", lf.at[0, z, k, xh])
        sent(("l", 0), lf.at[0, pl.ds(0, NZ - 1), k])
        sent(("l", 1), lf.at[1, pl.ds(0, NZ - 1), k, xh])
        sent(("lx", 1), lf.at[1, :, k, xh])
        for s in range(2):
            sent(("lk", s), lf.at[s, :, k])

    def r_send(g):
        blk = rhs.at[g, xl, y]
        send(("rx", g), None, blk, blk, dev(dxl=1))
        send(("ry", g), ("+", 0), blk, blk, dev(dy=1))
        send(("ry", g), ("-", 0), blk, blk, dev(dy=3))

    def r_other(g):
        blk = rhs.at[g, 1 - xl, y]
        recv(("rx", g), None, blk, dev(dxl=1))
        send(("ry", g), ("+", 1), blk, blk, dev(dy=1))
        send(("ry", g), ("-", 1), blk, blk, dev(dy=3))

    def r_forward(g):
        for j in range(2):
            which = xl if j == 0 else 1 - xl
            recv(("ry", g), ("+", j), rhs.at[g, which, (y + 3) % NY], dev(dy=3))
            if j == 0:
                blk = rhs.at[g, which, (y + 3) % NY]
                send(("rf", g), (j,), blk, blk, dev(dy=1))
            recv(("ry", g), ("-", j), rhs.at[g, which, (y + 1) % NY], dev(dy=1))
            if j == 1:
                blk = rhs.at[g, which, (y + 1) % NY]
                send(("rf", g), (j,), blk, blk, dev(dy=3))

    def r_done(g):
        far = (y + 2) % NY
        recv(("rf", g), (0,), rhs.at[g, xl, far], dev(dy=3))
        recv(("rf", g), (1,), rhs.at[g, 1 - xl, far], dev(dy=1))

    def r_sent(g):
        sent(("rx", g), rhs.at[g, xl, y])
        sent(("ry", g), rhs.at[g, xl])
        sent(("rf", g), rhs.at[g, xl, pl.ds(0, 2)])

    places = [(a, c, b) for a in range(NZ) for b in range(2) for c in range(2)]

    def weights(s, which, two):
        halves = [
            jnp.concatenate([tab[s, c, a, 2 * two + j, b, 16 * which:16 * which + 16, :] for a, c, b in places], axis=0)
            for j in range(2)
        ]
        return split(jnp.concatenate(halves, axis=1))

    def solve(s):
        top = split(jnp.concatenate([rhs[s, 0, j] for j in range(4)], axis=1))
        for two in range(2):
            out = product(top, weights(s, 0, two))
            xs[s, 2 * two] = out[:, :128]
            xs[s, 2 * two + 1] = out[:, 128:]
        first = split(jnp.concatenate([xs[s, j] for j in range(4)], axis=1))
        rest = []
        for two in range(2):
            out = product(first, weights(s, 1, two))
            rest.append(rhs[s, 1, 2 * two] - out[:, :128])
            rest.append(rhs[s, 1, 2 * two + 1] - out[:, 128:])
        rest = split(jnp.concatenate(rest, axis=1))
        for two in range(2):
            out = product(rest, weights(s, 2, two))
            xs[s, 4 + 2 * two] = out[:, :128]
            xs[s, 5 + 2 * two] = out[:, 128:]

    def whole(s):
        return split(jnp.concatenate([xs[s, j] for j in range(8)], axis=1))

    def emit(s):
        xo[s] = xs[s, row].T
        copy = pltpu.make_async_copy(xo.at[s], x_out.at[s], os.at[s])
        copy.start()
        return copy

    d0, d1, d2, d3 = PAIRS
    t_zsend(0)
    rhs[0, xl, y] = bs[0].T
    r_send(0)
    t_x(0, d0)
    r_other(0)
    t_x(0, d1)
    t_x(0, d2)
    t_x(0, d3)
    for c in loads[8:10]:
        c.wait()
    own = lf.at[0, z, k, xh]
    send("l0x", None, own, own, dev(dxh=1))
    l_hop(1, 0)
    c_z()
    t_y(0, d0)
    r_forward(0)
    t_zsend(1)
    recv("l0x", None, lf.at[0, z, k, 1 - xh], dev(dxh=1))
    l_hop(0, 0)
    t_y(0, d1)
    t_f(0, d0)
    t_y(0, d2)
    t_f(0, d1)
    t_k(0, d0)
    c_x()
    t_y(0, d3)
    t_f(0, d2)
    t_k(0, d1)
    for d in PAIRS:
        t_x(1, d)
    t_f(0, d3)
    t_k(0, d2)
    l_hop(1, 1)
    l_cross(1, 0)
    t_y(1, d0)
    t_y(1, d1)
    c_k()
    t_k(0, d3)
    l_hop(0, 1)
    t_f(1, d0)
    r_done(0)
    t_done(0)
    c_done()
    solve(0)
    low_cross = split(jnp.concatenate([crs[c, b, a] for a, c, b in places], axis=0))
    rhs[1, xl, y] = bs[1].T - product(whole(0), low_cross)
    r_send(1)
    copies = [emit(0)]
    r_other(1)
    l_hop(1, 2)
    l_cross(1, 1)
    t_y(1, d2)
    t_f(1, d1)
    t_k(1, d0)
    r_forward(1)
    l_hop(0, 2)
    t_y(1, d3)
    t_f(1, d2)
    t_k(1, d1)
    t_f(1, d3)
    t_k(1, d2)
    l_hop(1, 3)
    l_cross(1, 2)
    t_k(1, d3)
    l_hop(0, 3)
    r_done(1)
    l_hop(1, 4)
    l_cross(1, 3)
    l_hop(0, 4)
    l_cross(1, 4)
    l_done(0)

    def tile(s, j):
        at = pl.ds(pl.multiple_of(j * 256, 256), 256)
        return split(jnp.concatenate([lf[s, a, c, b, :, at] for a, c, b in places], axis=0))

    first = whole(0)

    @pl.loop(0, 4)
    def _(j):
        acc[j] = product(first, tile(0, j))

    t_done(1)
    solve(1)
    copies.append(emit(1))
    l_done(1)
    second = whole(1)
    loads[10].wait()

    @pl.loop(0, 4)
    def _(j):
        at = pl.ds(pl.multiple_of(j * 256, 256), 256)
        to[at, :] = bt[at, :] - (acc[j] + product(second, tile(1, j))).T

    last = pltpu.make_async_copy(to, t_out, os.at[2])
    last.start()
    for c in copies:
        c.wait()
    last.wait()
    for g in range(2):
        t_sent(g)
        r_sent(g)
    c_sent()
    l_sent()
    assert len(ids) <= N_RECV and len(streams) <= N_SEND, (len(ids), len(streams))


def shards(b_steps, b_trail, cross, trail, inv, low):
    anywhere = pl.BlockSpec(memory_space=pl.ANY)
    return pl.pallas_call(
        kernel,
        out_shape=(
            jax.ShapeDtypeStruct((2, 128, 256), F32),
            jax.ShapeDtypeStruct((1024, 256), F32),
        ),
        in_specs=[anywhere] * 6,
        out_specs=(anywhere, anywhere),
        scratch_shapes=[
            pltpu.VMEM((2, NZ, 2, 2, 32, 1024), F32),
            pltpu.VMEM((2, 2, NZ, NY, 2, 48, 128), F32),
            pltpu.VMEM((2, 2, NZ, 32, 128), F32),
            pltpu.VMEM((2, 2, NY, 256, 128), F32),
            pltpu.VMEM((2, 8, 256, 128), F32),
            pltpu.VMEM((4, 256, 256), F32),
            pltpu.VMEM((2, 128, 256), F32),
            pltpu.VMEM((1024, 256), F32),
            pltpu.VMEM((2, 128, 256), F32),
            pltpu.VMEM((1024, 256), F32),
            pltpu.SemaphoreType.DMA((N_SEND,)),
            pltpu.SemaphoreType.DMA((N_RECV,)),
            pltpu.SemaphoreType.DMA((16,)),
            pltpu.SemaphoreType.DMA((4,)),
        ],
        compiler_params=pltpu.CompilerParams(
            collective_id=0, has_side_effects=True, vmem_limit_bytes=56 << 20),
    )(
        b_steps, b_trail, cross.T, jnp.swapaxes(trail, 1, 2),
        jnp.swapaxes(inv, 2, 3), jnp.swapaxes(low, 1, 2),
    )


def solution(mesh):
    placed = (
        P(None, "row", "col"),
        P("row", "col"),
        P("row", "col"),
        P(None, "row", "col"),
        P(None, None, None, "col"),
        P(None, None, "col"),
    )
    return jax.shard_map(
        shards,
        mesh=mesh,
        in_specs=placed,
        out_specs=(P(None, "row", "col"), P("row", "col")),
        check_vma=False,
    )
```

```python
import jax
import jax.numpy as jnp
from jax import lax
from jax.experimental import pallas as pl
from jax.experimental.pallas import tpu as pltpu
from jax.sharding import PartitionSpec as P

MESH = pl.DeviceIdType.MESH
F32 = jnp.float32
BF16 = jnp.bfloat16

NY, NZ = 4, 8
PAIRS = (0, 1, 3, 2)
N_SEND, N_RECV = 32, 128

ORDER = (
    ("tz", 0), ("first",), ("rs", 0), ("tx", 0, 0), ("tx", 0, 3), ("tx", 0, 1), ("load",), ("hop", 1, 0, -1), ("cz",),
    ("rf", 0, 0), ("ro", 0), ("tz", 1), ("tx", 0, 2), ("ty", 0, 0), ("ty", 0, 3), ("ty", 0, 1), ("hop", 1, 1, -1),
    ("hop", 1, 0, 1), ("tx", 1, 0), ("rf", 0, 1), ("tx", 1, 3), ("cx",), ("pair",), ("hop", 0, 0, 1),
    ("hop", 0, 0, -1), ("tf", 0, 0, -1), ("ty", 0, 2), ("tx", 1, 1), ("tf", 0, 3, -1), ("tf", 0, 0, 1), ("tx", 1, 2),
    ("cross", 1, 1, -1), ("tf", 0, 1, -1), ("hop", 1, 1, 1), ("tf", 0, 3, 1), ("hop", 1, 2, -1), ("tf", 0, 1, 1),
    ("cross", 1, 0, 1), ("ty", 1, 0), ("tf", 0, 2, 1), ("ty", 1, 3), ("hop", 0, 1, 1), ("tk", 0, 0), ("tf", 0, 2, -1),
    ("tk", 0, 3), ("tk", 0, 1), ("hop", 0, 1, -1), ("ck",), ("hop", 1, 2, 1), ("ty", 1, 1), ("tf", 1, 0, 1),
    ("tf", 1, 0, -1), ("ty", 1, 2), ("hop", 1, 3, -1), ("tf", 1, 3, -1), ("tf", 1, 3, 1), ("tk", 0, 2),
    ("cross", 1, 1, 1), ("hop", 0, 2, 1), ("tf", 1, 1, 1), ("tf", 1, 1, -1), ("next",), ("rs", 1), ("hop", 0, 2, -1),
    ("hop", 1, 3, 1), ("cross", 1, 2, -1), ("tk", 1, 0), ("tf", 1, 2, 1), ("hop", 1, 4, -1), ("tf", 1, 2, -1),
    ("tk", 1, 3), ("cross", 1, 2, 1), ("tk", 1, 1), ("hop", 0, 3, 1), ("cross", 1, 3, -1), ("rf", 1, 0), ("tk", 1, 2),
    ("ro", 1), ("hop", 0, 3, -1), ("cross", 1, 3, 1), ("hop", 0, 4, 1), ("rf", 1, 1), ("cross", 1, 4, -1), ("trail",),
    ("finish",),
)


def split(value):
    high = value.astype(BF16)
    return high, (value - high.astype(F32)).astype(BF16)


def product(left, right):
    dot = lambda a, b: jnp.dot(a, b, preferred_element_type=F32)
    return dot(left[0], right[0]) + (dot(left[0], right[1]) + dot(left[1], right[0]))


def kernel(
    b_steps, b_trail, cross, trail, inv, low,
    x_out, t_out,
    lf, tab, crs, rhs, xs, acc, bs, bt, xo, to,
    ss, rs, ls, os,
):
    row, col = lax.axis_index("row"), lax.axis_index("col")
    xl, y = row // NY, row % NY
    z, xh, k = col // 4, (col // 2) % 2, col % 2

    def dev(dxl=0, dy=0, dz=0, dxh=0, dk=0):
        a = (1 - xl) if dxl else xl
        b = (1 - xh) if dxh else xh
        c = (1 - k) if dk else k
        return (a * NY + (y + dy) % NY, ((z + dz) % NZ) * 4 + b * 2 + c)

    ids, streams = {}, {}

    def sem(name):
        return ids.setdefault(name, len(ids))

    def out_sem(stream):
        return streams.setdefault(stream, len(streams))

    def send(stream, at, src, dst, to_dev):
        pltpu.make_async_remote_copy(
            src_ref=src, dst_ref=dst, send_sem=ss.at[out_sem(stream)],
            recv_sem=rs.at[sem(stream) if at is None else sem((stream, at))],
            device_id=to_dev, device_id_type=MESH).start()

    def recv(stream, at, region, from_dev):
        i = sem(stream) if at is None else sem((stream, at)) if isinstance(at, tuple) else at
        pltpu.make_async_remote_copy(
            src_ref=region, dst_ref=region, send_sem=ss.at[out_sem(stream)], recv_sem=rs.at[i],
            device_id=from_dev, device_id_type=MESH).wait_recv()

    def sent(stream, region):
        pltpu.make_async_remote_copy(
            src_ref=region, dst_ref=region, send_sem=ss.at[streams[stream]], recv_sem=rs.at[0],
            device_id=dev(dk=1), device_id_type=MESH).wait_send()

    partners = [dev(dz=e) for e in range(1, NZ)] + [dev(dy=1), dev(dy=3), dev(dxl=1), dev(dxh=1), dev(dk=1)]
    barrier = pltpu.get_barrier_semaphore()
    for p in partners:
        pl.semaphore_signal(barrier, inc=1, device_id=p, device_id_type=MESH)
    loads = []

    def load(src, dst):
        copy = pltpu.make_async_copy(src, dst, ls.at[len(loads)])
        copy.start()
        loads.append(copy)

    lanes = pl.ds(pl.multiple_of(y * 128, 128), 128)
    load(b_steps, bs)
    load(cross, crs.at[k, xh, z])
    for s in range(2):
        mine = tab.at[s, k, z, y, xh]
        load(inv.at[s, 0, :, lanes], mine.at[pl.ds(0, 16)])
        load(low.at[s, :, lanes], mine.at[pl.ds(16, 16)])
        load(inv.at[s, 1, :, lanes], mine.at[pl.ds(32, 16)])
    for s in range(2):
        load(trail.at[s], lf.at[s, z, k, xh])
    load(b_trail, bt)
    for c in loads[:8]:
        c.wait()
    pl.semaphore_wait(barrier, len(partners))

    def pair(d):
        return (z // 2 + d) % (NZ // 2)

    tz = [[sem(("tz", g, e)) for e in range(NZ)] for g in range(2)]

    def t_zsend(g):
        blk = tab.at[g, k, z, y, xh]
        for e in range(1, NZ):
            pltpu.make_async_remote_copy(
                src_ref=blk, dst_ref=blk, send_sem=ss.at[out_sem(("tz", g))], recv_sem=rs.at[tz[g][e]],
                device_id=dev(dz=e), device_id_type=MESH).start()

    def t_x(g, d):
        zz = pair(d)
        for from_z in [2 * zz, 2 * zz + 1] if d else [z + 1 - 2 * (z % 2)]:
            e = (z - from_z + NZ) % NZ
            recv(("tz", g), tz[g][0] + e, tab.at[g, k, from_z, y, xh], dev(dz=1))
        blk = tab.at[g, k, pl.ds(2 * zz, 2), y, xh]
        send(("tx", g), (d,), blk, blk, dev(dxh=1))

    def t_y(g, d):
        zs = pl.ds(2 * pair(d), 2)
        recv(("tx", g), (d,), tab.at[g, k, zs, y, 1 - xh], dev(dxh=1))
        blk = tab.at[g, k, zs, y]
        send(("ty+", g), (d,), blk, blk, dev(dy=1))
        send(("ty-", g), (d,), blk, blk, dev(dy=3))

    def t_f(g, d, sign):
        zs = pl.ds(2 * pair(d), 2)
        name, near, half = ("+", (y + 3) % NY, 0) if sign > 0 else ("-", (y + 1) % NY, 1)
        recv(("ty" + name, g), (d,), tab.at[g, k, zs, near], dev(dy=NY - sign))
        blk = tab.at[g, k, zs, near, half]
        send(("tf" + name, g), (d,), blk, blk, dev(dy=sign % NY))

    def t_k(g, d):
        zs = pl.ds(2 * pair(d), 2)
        far = (y + 2) % NY
        recv(("tf+", g), (d,), tab.at[g, k, zs, far, 0], dev(dy=3))
        recv(("tf-", g), (d,), tab.at[g, k, zs, far, 1], dev(dy=1))
        blk = tab.at[g, k, zs]
        send(("tk", g), None, blk, blk, dev(dk=1))

    def t_done(g):
        recv(("tk", g), None, tab.at[g, 1 - k], dev(dk=1))

    def t_sent(g):
        sent(("tz", g), tab.at[g, k, pl.ds(0, NZ - 1), y, xh])
        sent(("tx", g), tab.at[g, k, :, y, xh])
        for sign in "+-":
            sent(("ty" + sign, g), tab.at[g, k, :, y])
            sent(("tf" + sign, g), tab.at[g, k, :, y, xh])
        sent(("tk", g), tab.at[g, k])

    def c_z():
        blk = crs.at[k, xh, z]
        for e in range(1, NZ):
            send("cz", None, blk, blk, dev(dz=e))

    def c_x():
        recv("cz", None, crs.at[k, xh, pl.ds(0, NZ - 1)], dev(dz=1))
        send("cx", None, crs.at[k, xh], crs.at[k, xh], dev(dxh=1))

    def c_k():
        recv("cx", None, crs.at[k, 1 - xh], dev(dxh=1))
        send("ck", None, crs.at[k], crs.at[k], dev(dk=1))

    def c_done():
        recv("ck", None, crs.at[1 - k], dev(dk=1))

    def c_sent():
        sent("cz", crs.at[k, xh, pl.ds(0, NZ - 1)])
        sent("cx", crs.at[k, xh])
        sent("ck", crs.at[k])

    def zrel(e):
        return (z + NZ - e) % NZ

    def l_load():
        for c in loads[8:10]:
            c.wait()
        own = lf.at[0, z, k, xh]
        send("l0x", None, own, own, dev(dxh=1))

    def l_pair():
        recv("l0x", None, lf.at[0, z, k, 1 - xh], dev(dxh=1))

    def l_hop(s, h, sign):
        at = zrel(h if sign > 0 else NZ - h)
        blk = lf.at[s, at, k] if s == 0 else lf.at[s, at, k, xh]
        if h:
            recv(("l", s), (sign, h), blk, dev(dz=NZ - sign))
        if h < (4 if (s == 0) == (sign > 0) else 3):
            send(("l", s), (sign, h + 1), blk, blk, dev(dz=sign % NZ))
        if h == 0 and sign < 0:
            return
        if s == 0:
            send(("lk", s), None, blk, blk, dev(dk=1))
        else:
            send(("lx", s), (sign * h,), blk, blk, dev(dxh=1))

    def l_cross(s, h, sign):
        at = zrel(h if sign > 0 else NZ - h)
        recv(("lx", s), (sign * h,), lf.at[s, at, k, 1 - xh], dev(dxh=1))
        blk = lf.at[s, at, k]
        send(("lk", s), None, blk, blk, dev(dk=1))

    def l_done(s):
        recv(("lk", s), None, lf.at[s, :, 1 - k], dev(dk=1))

    def l_sent():
        sent("l0x", lf.at[0, z, k, xh])
        sent(("l", 0), lf.at[0, pl.ds(0, NZ - 1), k])
        sent(("l", 1), lf.at[1, pl.ds(0, NZ - 1), k, xh])
        sent(("lx", 1), lf.at[1, :, k, xh])
        for s in range(2):
            sent(("lk", s), lf.at[s, :, k])

    def r_send(g):
        blk = rhs.at[g, xl, y]
        send(("rx", g), None, blk, blk, dev(dxl=1))
        send(("ry", g), ("+", 0), blk, blk, dev(dy=1))
        send(("ry", g), ("-", 0), blk, blk, dev(dy=3))

    def r_other(g):
        blk = rhs.at[g, 1 - xl, y]
        recv(("rx", g), None, blk, dev(dxl=1))
        send(("ry", g), ("+", 1), blk, blk, dev(dy=1))
        send(("ry", g), ("-", 1), blk, blk, dev(dy=3))

    def r_f(g, j):
        near, sign = ((y + 3) % NY, "+") if j == 0 else ((y + 1) % NY, "-")
        which = xl if j == 0 else 1 - xl
        blk = rhs.at[g, which, near]
        recv(("ry", g), (sign, j), blk, dev(dy=3 if j == 0 else 1))
        send(("rf", g), (j,), blk, blk, dev(dy=1 if j == 0 else 3))

    def r_done(g):
        far = (y + 2) % NY
        recv(("ry", g), ("-", 0), rhs.at[g, xl, (y + 1) % NY], dev(dy=1))
        recv(("ry", g), ("+", 1), rhs.at[g, 1 - xl, (y + 3) % NY], dev(dy=3))
        recv(("rf", g), (0,), rhs.at[g, xl, far], dev(dy=3))
        recv(("rf", g), (1,), rhs.at[g, 1 - xl, far], dev(dy=1))

    def r_sent(g):
        sent(("rx", g), rhs.at[g, xl, y])
        sent(("ry", g), rhs.at[g, xl])
        sent(("rf", g), rhs.at[g, xl, pl.ds(0, 2)])

    places = [(a, c, b) for a in range(NZ) for b in range(2) for c in range(2)]

    def weights(s, which, two):
        halves = [
            jnp.concatenate([tab[s, c, a, 2 * two + j, b, 16 * which:16 * which + 16, :] for a, c, b in places], axis=0)
            for j in range(2)
        ]
        return split(jnp.concatenate(halves, axis=1))

    def solve(s):
        top = split(jnp.concatenate([rhs[s, 0, j] for j in range(4)], axis=1))
        for two in range(2):
            out = product(top, weights(s, 0, two))
            xs[s, 2 * two] = out[:, :128]
            xs[s, 2 * two + 1] = out[:, 128:]
        first = split(jnp.concatenate([xs[s, j] for j in range(4)], axis=1))
        rest = []
        for two in range(2):
            out = product(first, weights(s, 1, two))
            rest.append(rhs[s, 1, 2 * two] - out[:, :128])
            rest.append(rhs[s, 1, 2 * two + 1] - out[:, 128:])
        rest = split(jnp.concatenate(rest, axis=1))
        for two in range(2):
            out = product(rest, weights(s, 2, two))
            xs[s, 4 + 2 * two] = out[:, :128]
            xs[s, 5 + 2 * two] = out[:, 128:]

    def whole(s):
        return split(jnp.concatenate([xs[s, j] for j in range(8)], axis=1))

    def emit(s):
        xo[s] = xs[s, row].T
        copy = pltpu.make_async_copy(xo.at[s], x_out.at[s], os.at[s])
        copy.start()
        return copy

    copies = []

    def tile(s, j):
        at = pl.ds(pl.multiple_of(j * 256, 256), 256)
        return split(jnp.concatenate([lf[s, a, c, b, :, at] for a, c, b in places], axis=0))

    def r_first():
        rhs[0, xl, y] = bs[0].T

    def r_next():
        r_done(0)
        t_done(0)
        c_done()
        solve(0)
        low_cross = split(jnp.concatenate([crs[c, b, a] for a, c, b in places], axis=0))
        rhs[1, xl, y] = bs[1].T - product(whole(0), low_cross)

    def trail_first():
        copies.append(emit(0))
        l_done(0)
        first = whole(0)

        @pl.loop(0, 4)
        def _(j):
            acc[j] = product(first, tile(0, j))

    def finish():
        r_done(1)
        t_done(1)
        solve(1)
        copies.append(emit(1))
        l_done(1)
        second = whole(1)
        loads[10].wait()

        @pl.loop(0, 4)
        def _(j):
            at = pl.ds(pl.multiple_of(j * 256, 256), 256)
            to[at, :] = bt[at, :] - (acc[j] + product(second, tile(1, j))).T

        copies.append(pltpu.make_async_copy(to, t_out, os.at[2]))
        copies[-1].start()
        for c in copies:
            c.wait()

    for step, *at in ORDER:
        {
            "tz": t_zsend, "tx": t_x, "ty": t_y, "tf": t_f, "tk": t_k, "cz": c_z, "cx": c_x, "ck": c_k,
            "load": l_load, "pair": l_pair, "hop": l_hop, "cross": l_cross, "rs": r_send, "ro": r_other, "rf": r_f,
            "first": r_first, "next": r_next, "trail": trail_first, "finish": finish,
        }[step](*at)
    for g in range(2):
        t_sent(g)
        r_sent(g)
    c_sent()
    l_sent()
    assert len(ids) <= N_RECV and len(streams) <= N_SEND, (len(ids), len(streams))


def shards(b_steps, b_trail, cross, trail, inv, low):
    anywhere = pl.BlockSpec(memory_space=pl.ANY)
    return pl.pallas_call(
        kernel,
        out_shape=(
            jax.ShapeDtypeStruct((2, 128, 256), F32),
            jax.ShapeDtypeStruct((1024, 256), F32),
        ),
        in_specs=[anywhere] * 6,
        out_specs=(anywhere, anywhere),
        scratch_shapes=[
            pltpu.VMEM((2, NZ, 2, 2, 32, 1024), F32),
            pltpu.VMEM((2, 2, NZ, NY, 2, 48, 128), F32),
            pltpu.VMEM((2, 2, NZ, 32, 128), F32),
            pltpu.VMEM((2, 2, NY, 256, 128), F32),
            pltpu.VMEM((2, 8, 256, 128), F32),
            pltpu.VMEM((4, 256, 256), F32),
            pltpu.VMEM((2, 128, 256), F32),
            pltpu.VMEM((1024, 256), F32),
            pltpu.VMEM((2, 128, 256), F32),
            pltpu.VMEM((1024, 256), F32),
            pltpu.SemaphoreType.DMA((N_SEND,)),
            pltpu.SemaphoreType.DMA((N_RECV,)),
            pltpu.SemaphoreType.DMA((16,)),
            pltpu.SemaphoreType.DMA((4,)),
        ],
        compiler_params=pltpu.CompilerParams(
            collective_id=0, has_side_effects=True, vmem_limit_bytes=56 << 20),
    )(
        b_steps, b_trail, cross.T, jnp.swapaxes(trail, 1, 2),
        jnp.swapaxes(inv, 2, 3), jnp.swapaxes(low, 1, 2),
    )


def solution(mesh):
    placed = (
        P(None, "row", "col"),
        P("row", "col"),
        P("row", "col"),
        P(None, "row", "col"),
        P(None, None, None, "col"),
        P(None, None, "col"),
    )
    return jax.shard_map(
        shards,
        mesh=mesh,
        in_specs=placed,
        out_specs=(P(None, "row", "col"), P("row", "col")),
        check_vma=False,
    )
```

```python
import jax
import jax.numpy as jnp
from jax import lax
from jax.experimental import pallas as pl
from jax.experimental.pallas import tpu as pltpu
from jax.sharding import PartitionSpec as P

MESH = pl.DeviceIdType.MESH
F32 = jnp.float32
BF16 = jnp.bfloat16

NY, NZ = 4, 8
PAIRS = (0, 1, 3, 2)
N_SEND, N_RECV = 72, 136

ORDER = (
    ("tz", 0), ("first",), ("rs", 0), ("cz",), ("tx", 0, 0), ("tx", 0, 3), ("tx", 0, 1), ("ro", 0, 0), ("tx", 0, 2),
    ("r0", 0), ("ro", 0, 1), ("ty", 0, 0), ("load",), ("hop", 1, 0, -1), ("tz", 1), ("r1", 0, 0), ("ty", 0, 3),
    ("hop", 1, 0, 1), ("cx",), ("ty", 0, 1), ("r1", 0, 1), ("ty", 0, 2), ("tx", 1, 0), ("tx", 1, 3), ("tf", 0, 0, -1),
    ("hop", 1, 1, -1), ("pair",), ("hop", 0, 0, -1), ("hop", 0, 0, 1), ("tx", 1, 1), ("tf", 0, 0, 1),
    ("tf", 0, 3, -1), ("tx", 1, 2), ("tf", 0, 3, 1), ("hop", 1, 1, 1), ("tf", 0, 1, -1), ("cross", 1, 0, 1),
    ("tf", 0, 1, 1), ("hop", 1, 2, -1), ("tf", 0, 2, 1), ("tf", 0, 2, -1), ("ck",), ("tk", 0, 0), ("ty", 1, 0),
    ("tk", 0, 3), ("ty", 1, 3), ("hop", 0, 1, 1), ("tk", 0, 1), ("tk", 0, 2), ("hop", 0, 1, -1), ("tf", 1, 0, 1),
    ("cross", 1, 1, -1), ("hop", 1, 2, 1), ("tf", 1, 0, -1), ("ty", 1, 1), ("next",), ("rs", 1), ("hop", 1, 3, -1),
    ("tk", 1, 0), ("tf", 1, 3, 1), ("ty", 1, 2), ("tf", 1, 3, -1), ("trail", 0), ("cross", 1, 1, 1), ("tf", 1, 1, -1),
    ("tf", 1, 1, 1), ("hop", 0, 2, 1), ("trail", 1), ("r0", 1), ("hop", 0, 2, -1), ("hop", 1, 3, 1),
    ("cross", 1, 2, -1), ("tf", 1, 2, -1), ("tf", 1, 2, 1), ("hop", 1, 4, -1), ("tk", 1, 3), ("cross", 1, 2, 1),
    ("tk", 1, 1), ("ro", 1, 0), ("hop", 0, 3, 1), ("ro", 1, 1), ("tk", 1, 2), ("r1", 1, 0), ("trail", 2),
    ("hop", 0, 3, -1), ("cross", 1, 3, -1), ("r1", 1, 1), ("cross", 1, 3, 1), ("hop", 0, 4, 1), ("cross", 1, 4, -1),
    ("trail", 3), ("finish",),
)


def split(value):
    high = value.astype(BF16)
    return high, (value - high.astype(F32)).astype(BF16)


def product(left, right):
    dot = lambda a, b: jnp.dot(a, b, preferred_element_type=F32)
    return dot(left[0], right[0]) + (dot(left[0], right[1]) + dot(left[1], right[0]))


def kernel(
    b_steps, b_trail, cross, trail, inv, low,
    x_out, t_out,
    lf, tab, crs, rhs, xs, acc, bs, bt,
    ss, rs, ls,
):
    row, col = lax.axis_index("row"), lax.axis_index("col")
    xl, y = lax.div(row, NY), lax.rem(row, NY)
    z, xh, k = lax.div(col, 4), lax.rem(lax.div(col, 2), 2), lax.rem(col, 2)
    ys = [lax.rem(y + i, NY) for i in range(NY)]
    zs_at = [lax.rem(z + i, NZ) for i in range(NZ)]
    pairs = [lax.rem(lax.div(z, 2) + i, NZ // 2) for i in range(NZ // 2)]
    beside = z + 1 - 2 * lax.rem(z, 2)

    def dev(dxl=0, dy=0, dz=0, dxh=0, dk=0):
        a = (1 - xl) if dxl else xl
        b = (1 - xh) if dxh else xh
        c = (1 - k) if dk else k
        return (a * NY + ys[dy % NY], zs_at[dz % NZ] * 4 + b * 2 + c)

    ids, streams = {}, {}

    def sem(name):
        return ids.setdefault(name, len(ids))

    def out_sem(stream):
        return streams.setdefault(stream, len(streams))

    def send(stream, at, src, dst, to_dev):
        pltpu.make_async_remote_copy(
            src_ref=src, dst_ref=dst, send_sem=ss.at[out_sem(stream)],
            recv_sem=rs.at[sem(stream) if at is None else sem((stream, at))],
            device_id=to_dev, device_id_type=MESH).start()

    def recv(stream, at, region, from_dev):
        i = sem(stream) if at is None else sem((stream, at)) if isinstance(at, tuple) else at
        pltpu.make_async_remote_copy(
            src_ref=region, dst_ref=region, send_sem=ss.at[out_sem(stream)], recv_sem=rs.at[i],
            device_id=from_dev, device_id_type=MESH).wait_recv()

    def sent(stream, region):
        pltpu.make_async_remote_copy(
            src_ref=region, dst_ref=region, send_sem=ss.at[streams[stream]], recv_sem=rs.at[0],
            device_id=dev(dk=1), device_id_type=MESH).wait_send()

    partners = [dev(dz=e) for e in range(1, NZ)] + [dev(dy=1), dev(dy=3), dev(dxl=1), dev(dxh=1), dev(dk=1)]
    barrier = pltpu.get_barrier_semaphore()
    for p in partners:
        pl.semaphore_signal(barrier, inc=1, device_id=p, device_id_type=MESH)
    loads = []

    def load(src, dst):
        copy = pltpu.make_async_copy(src, dst, ls.at[len(loads)])
        copy.start()
        loads.append(copy)

    lanes = pl.ds(pl.multiple_of(y * 128, 128), 128)
    load(b_steps, bs)
    load(cross, crs.at[k, xh, z])
    for s in range(2):
        mine = tab.at[s, k, z, y, xh]
        load(inv.at[s, 0, :, lanes], mine.at[pl.ds(0, 16)])
        load(low.at[s, :, lanes], mine.at[pl.ds(16, 16)])
        load(inv.at[s, 1, :, pl.ds(pl.multiple_of((NY - 1 - y) * 128, 128), 128)], mine.at[pl.ds(32, 16)])
    for s in range(2):
        load(trail.at[s], lf.at[s, z, k, xh])
    load(b_trail, bt)
    for c in loads[:8]:
        c.wait()
    pl.semaphore_wait(barrier, len(partners))

    def filled(zz, at_y, act):
        p, q = zz <= at_y, zz <= NY - 1 - at_y
        for rows, when in (
            (pl.ds(0, 48), p & q),
            (pl.ds(0, 32), p & (zz > NY - 1 - at_y)),
            (pl.ds(16, 32), (zz > at_y) & q),
            (pl.ds(16, 16), (zz > at_y) & (zz > NY - 1 - at_y)),
        ):
            pl.when(when)(lambda rows=rows: act(rows))

    def pair(d):
        return pairs[d]

    tz = [[sem(("tz", g, e)) for e in range(NZ)] for g in range(2)]

    def t_zsend(g):
        def act(rows):
            blk = tab.at[g, k, z, y, xh, rows]
            for e in range(1, NZ):
                pltpu.make_async_remote_copy(
                    src_ref=blk, dst_ref=blk, send_sem=ss.at[out_sem(("tz", g))], recv_sem=rs.at[tz[g][e]],
                    device_id=dev(dz=e), device_id_type=MESH).start()
        filled(pairs[0], y, act)

    def t_x(g, d):
        def act(rows):
            zz = pair(d)
            for from_z in [2 * zz, 2 * zz + 1] if d else [beside]:
                e = lax.rem(z - from_z + NZ, NZ)
                recv(("tz", g), tz[g][0] + e, tab.at[g, k, from_z, y, xh, rows], dev(dz=1))
            blk = tab.at[g, k, pl.ds(2 * zz, 2), y, xh, rows]
            send(("tx", g, d), None, blk, blk, dev(dxh=1))
        filled(pair(d), y, act)

    def t_y(g, d):
        zs = pl.ds(2 * pair(d), 2)

        def act(rows):
            recv(("tx", g, d), None, tab.at[g, k, zs, y, 1 - xh, rows], dev(dxh=1))
            blk = tab.at[g, k, zs, y, :, rows]
            send(("ty+", g, d), None, blk, blk, dev(dy=1))
            send(("ty-", g, d), None, blk, blk, dev(dy=3))
        filled(pair(d), y, act)

    def t_f(g, d, sign):
        zs = pl.ds(2 * pair(d), 2)
        name, near, half = ("+", ys[3], 0) if sign > 0 else ("-", ys[1], 1)

        def act(rows):
            recv(("ty" + name, g, d), None, tab.at[g, k, zs, near, :, rows], dev(dy=NY - sign))
            blk = tab.at[g, k, zs, near, half, rows]
            send(("tf" + name, g, d), None, blk, blk, dev(dy=sign % NY))
        filled(pair(d), near, act)

    def t_k(g, d):
        zs = pl.ds(2 * pair(d), 2)
        far = ys[2]

        def act(rows):
            recv(("tf+", g, d), None, tab.at[g, k, zs, far, 0, rows], dev(dy=3))
            recv(("tf-", g, d), None, tab.at[g, k, zs, far, 1, rows], dev(dy=1))
        filled(pair(d), far, act)
        blk = tab.at[g, k, zs]
        send(("tk", g), None, blk, blk, dev(dk=1))

    def t_done(g):
        recv(("tk", g), None, tab.at[g, 1 - k], dev(dk=1))

    def t_sent(g):
        filled(pairs[0], y, lambda rows: sent(("tz", g), tab.at[g, k, pl.ds(0, NZ - 1), y, xh, rows]))
        for d in PAIRS:
            zs = pl.ds(2 * pair(d), 2)

            def act(rows):
                sent(("tx", g, d), tab.at[g, k, zs, y, xh, rows])
                sent(("ty+", g, d), tab.at[g, k, zs, y, :, rows])
                sent(("ty-", g, d), tab.at[g, k, zs, y, :, rows])
            filled(pair(d), y, act)
            for name, near in (("+", ys[3]), ("-", ys[1])):
                filled(pair(d), near, lambda rows: sent(("tf" + name, g, d), tab.at[g, k, zs, near, 0, rows]))
        sent(("tk", g), tab.at[g, k])

    def c_z():
        blk = crs.at[k, xh, z]
        for e in range(1, NZ):
            send("cz", None, blk, blk, dev(dz=e))

    def c_x():
        recv("cz", None, crs.at[k, xh, pl.ds(0, NZ - 1)], dev(dz=1))
        send("cx", None, crs.at[k, xh], crs.at[k, xh], dev(dxh=1))

    def c_k():
        recv("cx", None, crs.at[k, 1 - xh], dev(dxh=1))
        send("ck", None, crs.at[k], crs.at[k], dev(dk=1))

    def c_done():
        recv("ck", None, crs.at[1 - k], dev(dk=1))

    def c_sent():
        sent("cz", crs.at[k, xh, pl.ds(0, NZ - 1)])
        sent("cx", crs.at[k, xh])
        sent("ck", crs.at[k])

    def zrel(e):
        return zs_at[-e % NZ]

    def l_load():
        for c in loads[8:10]:
            c.wait()
        own = lf.at[0, z, k, xh]
        send("l0x", None, own, own, dev(dxh=1))

    def l_pair():
        recv("l0x", None, lf.at[0, z, k, 1 - xh], dev(dxh=1))

    def l_hop(s, h, sign):
        at = zrel(h if sign > 0 else NZ - h)
        blk = lf.at[s, at, k] if s == 0 else lf.at[s, at, k, xh]
        if h:
            recv(("l", s), (sign, h), blk, dev(dz=NZ - sign))
        if h < (4 if (s == 0) == (sign > 0) else 3):
            send(("l", s), (sign, h + 1), blk, blk, dev(dz=sign % NZ))
        if h == 0 and sign < 0:
            return
        if s == 0:
            send(("lk", s), (sign * h,), blk, blk, dev(dk=1))
        else:
            send(("lx", s), (sign * h,), blk, blk, dev(dxh=1))

    def l_cross(s, h, sign):
        at = zrel(h if sign > 0 else NZ - h)
        recv(("lx", s), (sign * h,), lf.at[s, at, k, 1 - xh], dev(dxh=1))
        blk = lf.at[s, at, k]
        send(("lk", s), None, blk, blk, dev(dk=1))

    def l_done(s):
        recv(("lk", s), None, lf.at[s, :, 1 - k], dev(dk=1))

    def l_sent():
        sent("l0x", lf.at[0, z, k, xh])
        sent(("l", 0), lf.at[0, pl.ds(0, NZ - 1), k])
        sent(("l", 1), lf.at[1, pl.ds(0, NZ - 1), k, xh])
        sent(("lx", 1), lf.at[1, :, k, xh])
        for s in range(2):
            sent(("lk", s), lf.at[s, :, k])

    def r_send(g):
        for h in range(2):
            blk = rhs.at[g, xl, y, h]
            send(("rx", g), (h,), blk, blk, dev(dxl=1))
        blk = rhs.at[g, xl, y]
        send(("ry", g), ("+",), blk, blk, dev(dy=1))
        send(("ry", g), ("-",), blk, blk, dev(dy=3))

    def r_other(g, h):
        blk = rhs.at[g, 1 - xl, y, h]
        recv(("rx", g), (h,), blk, dev(dxl=1))
        send(("ro", g), ("+", h), blk, blk, dev(dy=1))
        send(("ro", g), ("-", h), blk, blk, dev(dy=3))

    def r_f0(g):
        blk = rhs.at[g, xl, ys[3]]
        recv(("ry", g), ("+",), blk, dev(dy=3))
        send(("rf", g), None, blk, blk, dev(dy=1))

    def r_f1(g, h):
        blk = rhs.at[g, 1 - xl, ys[1], h]
        recv(("ro", g), ("-", h), blk, dev(dy=1))
        send(("rg", g), (h,), blk, blk, dev(dy=3))

    def r_done(g):
        far = ys[2]
        recv(("ry", g), ("-",), rhs.at[g, xl, ys[1]], dev(dy=1))
        recv(("rf", g), None, rhs.at[g, xl, far], dev(dy=3))
        for h in range(2):
            recv(("ro", g), ("+", h), rhs.at[g, 1 - xl, ys[3], h], dev(dy=3))
            recv(("rg", g), (h,), rhs.at[g, 1 - xl, far, h], dev(dy=1))

    def r_sent(g):
        sent(("rx", g), rhs.at[g, xl, y])
        sent(("ry", g), rhs.at[g, xl, pl.ds(0, 2)])
        sent(("ro", g), rhs.at[g, xl, pl.ds(0, 2)])
        sent(("rf", g), rhs.at[g, xl, y])
        sent(("rg", g), rhs.at[g, xl, y])

    places = [(a, c, b) for a in range(NZ) for b in range(2) for c in range(2)]

    def weights(s, which, two):
        deep = NZ if which == 1 else 4 * two + 4
        halves = []
        for m in (2 * two, 2 * two + 1):
            at = NY - 1 - m if which == 2 else m
            halves.append(jnp.concatenate([
                tab[s, c, a, at, b, 16 * which:16 * which + 16, :] if which == 1 or a // 2 <= m
                else jnp.zeros((16, 128), F32)
                for a, c, b in places if a < deep], axis=0))
        return split(jnp.concatenate(halves, axis=1))

    def part(pair_of, two):
        return tuple(v[:, :256 * two + 256] for v in pair_of)

    def blocks(g, x):
        return [rhs[g, x, j].reshape(256, 128) for j in range(NY)]

    def solve(s):
        top = split(jnp.concatenate(blocks(s, 0), axis=1))
        out = [product(part(top, two), weights(s, 0, two)) for two in range(2)]
        for j in range(4):
            xs[s, j] = out[j // 2][:, 128 * (j % 2):128 * (j % 2) + 128]
        first = split(jnp.concatenate(out, axis=1))
        out = [product(first, weights(s, 1, two)) for two in range(2)]
        rest = split(jnp.concatenate(blocks(s, 1), axis=1) - jnp.concatenate(out, axis=1))
        out = [product(part(rest, two), weights(s, 2, two)) for two in range(2)]
        for j in range(4):
            xs[s, 4 + j] = out[j // 2][:, 128 * (j % 2):128 * (j % 2) + 128]

    def whole(s):
        return split(jnp.concatenate([xs[s, j] for j in range(8)], axis=1))

    def emit(s):
        x_out[s] = xs[s, row].T

    def r_first():
        rhs[0, xl, y] = bs[0].T.reshape(2, 128, 128)

    def r_next():
        r_done(0)
        t_done(0)
        c_done()
        solve(0)
        low_cross = split(jnp.concatenate([crs[c, b, a] for a, c, b in places], axis=0))
        rhs[1, xl, y] = (bs[1].T - product(whole(0), low_cross)).reshape(2, 128, 128)

    def trail_first(i):
        if i == 0:
            emit(0)
        ats = []
        for h in (-i, i + 1):
            at = zrel(h if h >= 0 else NZ + h)
            recv(("lk", 0), (h,), lf.at[0, at, 1 - k], dev(dk=1))
            ats.append(at)
        first = split(jnp.concatenate([xs[0, at] for at in ats], axis=1))

        @pl.loop(0, 4)
        def _(j):
            lane = pl.ds(pl.multiple_of(j * 256, 256), 256)
            right = split(jnp.concatenate([lf[0, at, c, b, :, lane] for at in ats for b in range(2) for c in range(2)], axis=0))
            out = product(first, right)
            acc[j] = out if i == 0 else acc[j] + out

    def finish():
        r_done(1)
        t_done(1)
        solve(1)
        emit(1)
        l_done(1)
        second = whole(1)
        loads[10].wait()
        for j in range(4):
            at = slice(256 * j, 256 * j + 256)
            right = split(jnp.concatenate([lf[1, a, c, b, :, at] for a, c, b in places], axis=0))
            t_out[at, :] = bt[at, :] - (acc[j] + product(second, right)).T

    for step, *at in ORDER:
        {
            "tz": t_zsend, "tx": t_x, "ty": t_y, "tf": t_f, "tk": t_k, "cz": c_z, "cx": c_x, "ck": c_k,
            "load": l_load, "pair": l_pair, "hop": l_hop, "cross": l_cross, "rs": r_send, "ro": r_other, "r0": r_f0, "r1": r_f1,
            "first": r_first, "next": r_next, "trail": trail_first, "finish": finish,
        }[step](*at)
    for g in range(2):
        t_sent(g)
        r_sent(g)
    c_sent()
    l_sent()
    assert len(ids) <= N_RECV and len(streams) <= N_SEND, (len(ids), len(streams))


def shards(b_steps, b_trail, cross, trail, inv, low):
    anywhere = pl.BlockSpec(memory_space=pl.ANY)
    return pl.pallas_call(
        kernel,
        out_shape=(pltpu.VMEM((2, 128, 256), F32), pltpu.VMEM((1024, 256), F32)),
        in_specs=[anywhere] * 6,
        out_specs=(pl.BlockSpec(memory_space=pltpu.VMEM), pl.BlockSpec(memory_space=pltpu.VMEM)),
        scratch_shapes=[
            pltpu.VMEM((2, NZ, 2, 2, 32, 1024), F32),
            pltpu.VMEM((2, 2, NZ, NY, 2, 48, 128), F32),
            pltpu.VMEM((2, 2, NZ, 32, 128), F32),
            pltpu.VMEM((2, 2, NY, 2, 128, 128), F32),
            pltpu.VMEM((2, 8, 256, 128), F32),
            pltpu.VMEM((4, 256, 256), F32),
            pltpu.VMEM((2, 128, 256), F32),
            pltpu.VMEM((1024, 256), F32),
            pltpu.SemaphoreType.DMA((N_SEND,)),
            pltpu.SemaphoreType.DMA((N_RECV,)),
            pltpu.SemaphoreType.DMA((11,)),
        ],
        compiler_params=pltpu.CompilerParams(
            collective_id=0, has_side_effects=True, vmem_limit_bytes=57 << 20),
    )(
        b_steps, b_trail, cross.T, jnp.swapaxes(trail, 1, 2),
        jnp.swapaxes(inv, 2, 3), jnp.swapaxes(low, 1, 2),
    )


def solution(mesh):
    placed = (
        P(None, "row", "col"),
        P("row", "col"),
        P("row", "col"),
        P(None, "row", "col"),
        P(None, None, None, "col"),
        P(None, None, "col"),
    )
    return jax.shard_map(
        shards,
        mesh=mesh,
        in_specs=placed,
        out_specs=(P(None, "row", "col"), P("row", "col")),
        check_vma=False,
    )
```

```python
import jax
import jax.numpy as jnp
from jax import lax
from jax.experimental import pallas as pl
from jax.experimental.pallas import tpu as pltpu
from jax.sharding import PartitionSpec as P

MESH = pl.DeviceIdType.MESH
F32 = jnp.float32
BF16 = jnp.bfloat16

NY, NZ = 4, 8
PAIRED = (-1,)
PAIRS = (0, 1, 3, 2)
N_SEND, N_RECV = 72, 128

ORDER = (
    ("tz",), ("first",), ("rs", 0), ("ring", 0, -1), ("load",), ("hop", 1, 0, -1), ("ring", 0, 1), ("tx", 0, 0),
    ("tx", 0, 3), ("tx", 0, 1), ("ro", 0, 0), ("tx", 0, 2), ("r0", 0), ("ro", 0, 1), ("ring", 1, 1), ("ring", 1, -1),
    ("tx", 1, 0), ("r1", 0, 0), ("ring", 2, 1), ("hop", 1, 0, 1), ("pair",), ("hop", 0, 0, -1), ("r1", 0, 1),
    ("ty", 0, 0), ("ring", 2, -1), ("ty", 0, 3), ("ring", 3, 1), ("tx", 1, 3), ("ty", 0, 1), ("hop", 0, 0, 1),
    ("ty", 0, 2), ("ty", 1, 0), ("tf", 0, 0, 1), ("hop", 1, 1, -1), ("tf", 0, 0, -1), ("hop", 1, 1, 1),
    ("ring", 4, 1), ("tf", 0, 3, 1), ("tf", 0, 3, -1), ("cross", 1, 0, 1), ("hop", 0, 1, -1), ("tf", 0, 1, 1),
    ("ring", 3, -1), ("cx",), ("tx", 1, 1), ("tf", 0, 1, -1), ("ty", 1, 3), ("tx", 1, 2), ("tf", 0, 2, 1),
    ("tf", 0, 2, -1), ("tf", 1, 0, 1), ("hop", 1, 2, -1), ("cross", 1, 1, 1), ("tf", 1, 0, -1), ("hop", 0, 1, 1),
    ("tk", 0, 0), ("tk", 0, 3), ("cross", 1, 1, -1), ("tk", 0, 1), ("hop", 1, 2, 1), ("ck",), ("tf", 1, 3, 1),
    ("ty", 1, 1), ("tf", 1, 3, -1), ("ty", 1, 2), ("tk", 0, 2), ("tk", 1, 0), ("next",), ("rs", 1), ("hop", 0, 2, 1),
    ("hop", 0, 2, -1), ("tk", 1, 3), ("cross", 1, 2, -1), ("tf", 1, 1, -1), ("tf", 1, 1, 1), ("tf", 1, 2, 1),
    ("tf", 1, 2, -1), ("trail", 0, 0), ("hop", 1, 3, -1), ("cross", 1, 2, 1), ("hop", 1, 3, 1), ("trail", 0, 1),
    ("ro", 1, 0), ("r0", 1), ("ro", 1, 1), ("tk", 1, 1), ("tk", 1, 2), ("hop", 0, 3, 1), ("hop", 0, 3, -1),
    ("r1", 1, 0), ("cross", 1, 3, -1), ("r1", 1, 1), ("trail", 0, 2), ("hop", 1, 4, -1), ("cross", 1, 3, 1),
    ("last",), ("trail", 1, 0), ("hop", 0, 4, 1), ("trail", 1, 1), ("cross", 1, 4, -1), ("trail", 1, 2),
    ("trail", 0, 3), ("finish",),
)


def split(value):
    high = value.astype(BF16)
    return high, (value - high.astype(F32)).astype(BF16)


def product(left, right):
    dot = lambda a, b: jnp.dot(a, b, preferred_element_type=F32)
    return dot(left[0], right[0]) + (dot(left[0], right[1]) + dot(left[1], right[0]))


def kernel(
    b_steps, b_trail, cross, trail, inv, low,
    x_out, t_out,
    lf, tab, crs, rhs, xs, acc, bs, bt,
    ss, rs, ls,
):
    row, col = lax.axis_index("row"), lax.axis_index("col")
    xl, y = lax.div(row, NY), lax.rem(row, NY)
    z, xh, k = lax.div(col, 4), lax.rem(lax.div(col, 2), 2), lax.rem(col, 2)
    ys = [lax.rem(y + i, NY) for i in range(NY)]
    zs_at = [lax.rem(z + i, NZ) for i in range(NZ)]
    pairs = [lax.rem(lax.div(z, 2) + i, NZ // 2) for i in range(NZ // 2)]
    beside = z + 1 - 2 * lax.rem(z, 2)

    places_of = {}

    def dev(dxl=0, dy=0, dz=0, dxh=0, dk=0):
        return places_of[dxl, dy % NY, dz % NZ, dxh, dk]

    def greet(dxl=0, dy=0, dz=0, dxh=0, dk=0):
        at_row = ((1 - xl) if dxl else xl) * NY + ys[dy]
        at_col = zs_at[dz] * 4 + ((1 - xh) if dxh else xh) * 2 + ((1 - k) if dk else k)
        places_of[dxl, dy, dz, dxh, dk] = (at_row, at_col)
        return at_row, at_col

    ids, streams = {}, {}

    def sem(name):
        return ids.setdefault(name, len(ids))

    def out_sem(stream):
        return streams.setdefault(stream, len(streams))

    def send(stream, at, src, dst, to_dev, rs_name=None):
        pltpu.make_async_remote_copy(
            src_ref=src, dst_ref=dst, send_sem=ss.at[out_sem(stream)],
            recv_sem=rs.at[sem(rs_name or (stream if at is None else (stream, at)))],
            device_id=to_dev, device_id_type=MESH).start()

    def recv(stream, at, region, from_dev):
        i = sem(stream) if at is None else sem((stream, at)) if isinstance(at, tuple) else at
        pltpu.make_async_remote_copy(
            src_ref=region, dst_ref=region, send_sem=ss.at[out_sem(stream)], recv_sem=rs.at[i],
            device_id=from_dev, device_id_type=MESH).wait_recv()

    def sent(stream, region):
        pltpu.make_async_remote_copy(
            src_ref=region, dst_ref=region, send_sem=ss.at[streams[stream]], recv_sem=rs.at[0],
            device_id=dev(dk=1), device_id_type=MESH).wait_send()

    partners = [greet(dz=e) for e in range(1, NZ)] + [greet(dy=1), greet(dy=3), greet(dxl=1), greet(dxh=1), greet(dk=1)]
    barrier = pltpu.get_barrier_semaphore()
    for p in partners:
        pl.semaphore_signal(barrier, inc=1, device_id=p, device_id_type=MESH)
    loads = []

    def load(src, dst):
        copy = pltpu.make_async_copy(src, dst, ls.at[len(loads)])
        copy.start()
        loads.append(copy)

    lanes = pl.ds(pl.multiple_of(y * 128, 128), 128)
    load(b_steps, bs)
    load(cross, crs.at[k, xh, z])
    for s in range(2):
        mine = tab.at[s, k, z, y, xh]
        load(inv.at[s, 0, :, lanes], mine.at[pl.ds(0, 16)])
        load(low.at[s, :, lanes], mine.at[pl.ds(16, 16)])
        load(inv.at[s, 1, :, pl.ds(pl.multiple_of((NY - 1 - y) * 128, 128), 128)], mine.at[pl.ds(32, 16)])
    for s in range(2):
        load(trail.at[s], lf.at[s, z, k, xh])
    load(b_trail, bt)
    for c in loads[:8]:
        c.wait()
    pl.semaphore_wait(barrier, len(partners))

    def filled(zz, at_y, act):
        p, q = zz <= at_y, zz <= NY - 1 - at_y
        lax.cond(
            p,
            lambda: lax.cond(q, lambda: act(pl.ds(0, 48)), lambda: act(pl.ds(0, 32))),
            lambda: lax.cond(q, lambda: act(pl.ds(16, 32)), lambda: act(pl.ds(16, 16))),
        )

    def pair(d):
        return pairs[d]

    tz = [sem(("tz", e)) for e in range(NZ)]

    def t_zsend():
        def act(rows):
            blk = tab.at[0, k, z, y, xh, rows]
            for e in range(1, NZ):
                pltpu.make_async_remote_copy(
                    src_ref=blk, dst_ref=blk, send_sem=ss.at[out_sem("tz")], recv_sem=rs.at[tz[e]],
                    device_id=dev(dz=e), device_id_type=MESH).start()
        filled(pairs[0], y, act)

    def ring(h, sign):
        at = zrel(h if sign > 0 else NZ - h)
        last = h == (4 if sign > 0 else 3)
        blk = crs.at[k, xh, at]
        if h:
            recv("cr", (sign, h), blk, dev(dz=NZ - sign))
        if not last:
            send("cr", (sign, h + 1), blk, blk, dev(dz=sign % NZ))

        def act(rows):
            blk = tab.at[1, k, at, y, xh, rows]
            if h:
                recv(("tr", sign), (h,), blk, dev(dz=NZ - sign))
            if not last:
                send(("tr", sign, h), None, blk, blk, dev(dz=sign % NZ), rs_name=(("tr", sign), (h + 1,)))
        filled(lax.div(at, 2), y, act)

    def t_x(g, d):
        def act(rows):
            zz = pair(d)
            for from_z in () if g else (2 * zz, 2 * zz + 1) if d else (beside,):
                e = lax.rem(z - from_z + NZ, NZ)
                recv("tz", tz[0] + e, tab.at[g, k, from_z, y, xh, rows], dev(dz=1))
            blk = tab.at[g, k, pl.ds(2 * zz, 2), y, xh, rows]
            send(("tx", g, d), None, blk, blk, dev(dxh=1))
        filled(pair(d), y, act)

    def t_y(g, d):
        zs = pl.ds(2 * pair(d), 2)

        def act(rows):
            recv(("tx", g, d), None, tab.at[g, k, zs, y, 1 - xh, rows], dev(dxh=1))
            blk = tab.at[g, k, zs, y, :, rows]
            send(("ty+", g, d), None, blk, blk, dev(dy=1))
            send(("ty-", g, d), None, blk, blk, dev(dy=3))
        filled(pair(d), y, act)

    def t_f(g, d, sign):
        zs = pl.ds(2 * pair(d), 2)
        name, near, half = ("+", ys[3], 0) if sign > 0 else ("-", ys[1], 1)

        def act(rows):
            recv(("ty" + name, g, d), None, tab.at[g, k, zs, near, :, rows], dev(dy=NY - sign))
            blk = tab.at[g, k, zs, near, half, rows]
            send(("tf" + name, g, d), None, blk, blk, dev(dy=sign % NY))
        filled(pair(d), near, act)

    def t_k(g, d):
        zs = pl.ds(2 * pair(d), 2)
        far = ys[2]

        def act(rows):
            recv(("tf+", g, d), None, tab.at[g, k, zs, far, 0, rows], dev(dy=3))
            recv(("tf-", g, d), None, tab.at[g, k, zs, far, 1, rows], dev(dy=1))
        filled(pair(d), far, act)
        blk = tab.at[g, k, zs]
        send(("tk", g), None, blk, blk, dev(dk=1))

    def t_done(g):
        recv(("tk", g), None, tab.at[g, 1 - k], dev(dk=1))

    def t_sent(g):
        if g == 0:
            filled(pairs[0], y, lambda rows: sent("tz", tab.at[g, k, pl.ds(0, NZ - 1), y, xh, rows]))
        else:
            for sign, last in ((1, 4), (-1, 3)):
                for h in range(last):
                    at = zrel(h if sign > 0 else NZ - h)
                    filled(lax.div(at, 2), y, lambda rows: sent(("tr", sign, h), tab.at[g, k, at, y, xh, rows]))
        for d in PAIRS:
            zs = pl.ds(2 * pair(d), 2)

            def act(rows):
                sent(("tx", g, d), tab.at[g, k, zs, y, xh, rows])
                sent(("ty+", g, d), tab.at[g, k, zs, y, :, rows])
                sent(("ty-", g, d), tab.at[g, k, zs, y, :, rows])
            filled(pair(d), y, act)
            for name, near in (("+", ys[3]), ("-", ys[1])):
                filled(pair(d), near, lambda rows: sent(("tf" + name, g, d), tab.at[g, k, zs, near, 0, rows]))
        sent(("tk", g), tab.at[g, k])

    def c_x():
        send("cx", None, crs.at[k, xh], crs.at[k, xh], dev(dxh=1))

    def c_k():
        recv("cx", None, crs.at[k, 1 - xh], dev(dxh=1))
        send("ck", None, crs.at[k], crs.at[k], dev(dk=1))

    def c_done():
        recv("ck", None, crs.at[1 - k], dev(dk=1))

    def c_sent():
        sent("cr", crs.at[k, xh, pl.ds(0, NZ - 1)])
        sent("cx", crs.at[k, xh])
        sent("ck", crs.at[k])

    def zrel(e):
        return zs_at[-e % NZ]

    def l_load():
        for c in loads[8:10]:
            c.wait()
        own = lf.at[0, z, k, xh]
        send("l0x", None, own, own, dev(dxh=1))

    def l_pair():
        recv("l0x", None, lf.at[0, z, k, 1 - xh], dev(dxh=1))

    def l_hop(s, h, sign):
        at = zrel(h if sign > 0 else NZ - h)
        blk = lf.at[s, at, k] if s == 0 else lf.at[s, at, k, xh]
        if h:
            recv(("l", s), (sign, h), blk, dev(dz=NZ - sign))
        if h < (4 if (s == 0) == (sign > 0) else 3):
            send(("l", s), (sign, h + 1), blk, blk, dev(dz=sign % NZ))
        if h == 0 and sign < 0:
            return
        if s == 0:
            send(("lk", s), (sign * h,), blk, blk, dev(dk=1))
        else:
            if not (h == 1 and sign in PAIRED):
                send(("lx", s), (sign * h,), blk, blk, dev(dxh=1))

    def l_cross(s, h, sign):
        at = zrel(h if sign > 0 else NZ - h)
        blk = lf.at[s, at, k, 1 - xh]
        if h == 1 and sign in PAIRED:
            recv("lp", (sign,), blk, dev(dz=NZ - sign))
        else:
            recv(("lx", s), (sign * h,), blk, dev(dxh=1))
        if h == 0:
            for side in PAIRED:
                send("lp", (side,), blk, blk, dev(dz=side % NZ))
        blk = lf.at[s, at, k]
        send(("lk", s), (sign * h,), blk, blk, dev(dk=1))

    def l_sent():
        sent("l0x", lf.at[0, z, k, xh])
        sent(("l", 0), lf.at[0, pl.ds(0, NZ - 1), k])
        sent(("l", 1), lf.at[1, pl.ds(0, NZ - 1), k, xh])
        sent(("lx", 1), lf.at[1, pl.ds(0, NZ - len(PAIRED)), k, xh])
        if PAIRED:
            sent("lp", lf.at[1, pl.ds(0, len(PAIRED)), k, xh])
        for s in range(2):
            sent(("lk", s), lf.at[s, :, k])

    def r_send(g):
        for h in range(2):
            blk = rhs.at[g, xl, y, h]
            send(("rx", g), (h,), blk, blk, dev(dxl=1))
        blk = rhs.at[g, xl, y]
        send(("ry", g), ("+",), blk, blk, dev(dy=1))
        send(("ry", g), ("-",), blk, blk, dev(dy=3))

    def r_other(g, h):
        blk = rhs.at[g, 1 - xl, y, h]
        recv(("rx", g), (h,), blk, dev(dxl=1))
        send(("ro", g), ("+", h), blk, blk, dev(dy=1))
        send(("ro", g), ("-", h), blk, blk, dev(dy=3))

    def r_f0(g):
        blk = rhs.at[g, xl, ys[3]]
        recv(("ry", g), ("+",), blk, dev(dy=3))
        send(("rf", g), None, blk, blk, dev(dy=1))

    def r_f1(g, h):
        blk = rhs.at[g, 1 - xl, ys[1], h]
        recv(("ro", g), ("-", h), blk, dev(dy=1))
        send(("rg", g), (h,), blk, blk, dev(dy=3))

    def r_done(g):
        far = ys[2]
        recv(("ry", g), ("-",), rhs.at[g, xl, ys[1]], dev(dy=1))
        recv(("rf", g), None, rhs.at[g, xl, far], dev(dy=3))
        for h in range(2):
            recv(("ro", g), ("+", h), rhs.at[g, 1 - xl, ys[3], h], dev(dy=3))
            recv(("rg", g), (h,), rhs.at[g, 1 - xl, far, h], dev(dy=1))

    def r_sent(g):
        sent(("rx", g), rhs.at[g, xl, y])
        sent(("ry", g), rhs.at[g, xl, pl.ds(0, 2)])
        sent(("ro", g), rhs.at[g, xl, pl.ds(0, 2)])
        sent(("rf", g), rhs.at[g, xl, y])
        sent(("rg", g), rhs.at[g, xl, y])

    places = [(a, c, b) for a in range(NZ) for b in range(2) for c in range(2)]

    def weights(s, which, two):
        deep = NZ if which == 1 else 4 * two + 4
        halves = []
        for m in (2 * two, 2 * two + 1):
            at = NY - 1 - m if which == 2 else m
            halves.append(jnp.concatenate([
                tab[s, c, a, at, b, 16 * which:16 * which + 16, :] if which == 1 or a // 2 <= m
                else jnp.zeros((16, 128), F32)
                for a, c, b in places if a < deep], axis=0))
        return split(jnp.concatenate(halves, axis=1))

    def part(pair_of, two):
        return tuple(v[:, :256 * two + 256] for v in pair_of)

    def blocks(g, x):
        return [rhs[g, x, j].reshape(256, 128) for j in range(NY)]

    def solve(s):
        top = split(jnp.concatenate(blocks(s, 0), axis=1))
        out = [product(part(top, two), weights(s, 0, two)) for two in range(2)]
        for j in range(4):
            xs[s, j] = out[j // 2][:, 128 * (j % 2):128 * (j % 2) + 128]
        first = split(jnp.concatenate(out, axis=1))
        out = [product(first, weights(s, 1, two)) for two in range(2)]
        rest = split(jnp.concatenate(blocks(s, 1), axis=1) - jnp.concatenate(out, axis=1))
        out = [product(part(rest, two), weights(s, 2, two)) for two in range(2)]
        for j in range(4):
            xs[s, 4 + j] = out[j // 2][:, 128 * (j % 2):128 * (j % 2) + 128]

    def whole(s):
        return split(jnp.concatenate([xs[s, j] for j in range(8)], axis=1))

    def emit(s):
        x_out[s] = xs[s, row].T

    def r_first():
        rhs[0, xl, y] = bs[0].T.reshape(2, 128, 128)

    def r_next():
        r_done(0)
        t_done(0)
        c_done()
        solve(0)
        low_cross = split(jnp.concatenate([crs[c, b, a] for a, c, b in places], axis=0))
        rhs[1, xl, y] = (bs[1].T - product(whole(0), low_cross)).reshape(2, 128, 128)

    def trail_part(s, i):
        ats = []
        for h in (-i, i + 1) if s == 0 else (i, -i - 1):
            at = zrel(h if h >= 0 else NZ + h)
            recv(("lk", s), (h,), lf.at[s, at, 1 - k], dev(dk=1))
            ats.append(at)
        return split(jnp.concatenate([xs[s, at] for at in ats], axis=1)), ats

    def right(s, ats, lane):
        return split(jnp.concatenate([lf[s, at, c, b, :, lane] for at in ats for b in range(2) for c in range(2)], axis=0))

    def trail(s, i):
        left, ats = trail_part(s, i)

        @pl.loop(0, 4)
        def _(j):
            out = product(left, right(s, ats, pl.ds(pl.multiple_of(j * 256, 256), 256)))
            acc[j] = out if s == 0 and i == 0 else acc[j] + out

    def solve_last():
        emit(0)
        r_done(1)
        t_done(1)
        solve(1)
        emit(1)
        loads[10].wait()

    def finish():
        left, ats = trail_part(1, 3)
        for j in range(4):
            at = slice(256 * j, 256 * j + 256)
            t_out[at, :] = bt[at, :] - (acc[j] + product(left, right(1, ats, at))).T

    for step, *at in ORDER:
        {
            "tz": t_zsend, "ring": ring, "tx": t_x, "ty": t_y, "tf": t_f, "tk": t_k, "cx": c_x, "ck": c_k,
            "load": l_load, "pair": l_pair, "hop": l_hop, "cross": l_cross, "rs": r_send, "ro": r_other, "r0": r_f0, "r1": r_f1,
            "first": r_first, "next": r_next, "trail": trail, "last": solve_last, "finish": finish,
        }[step](*at)
    for g in range(2):
        t_sent(g)
        r_sent(g)
    c_sent()
    l_sent()
    assert len(ids) <= N_RECV and len(streams) <= N_SEND, (len(ids), len(streams))


def shards(b_steps, b_trail, cross, trail, inv, low):
    anywhere = pl.BlockSpec(memory_space=pl.ANY)
    return pl.pallas_call(
        kernel,
        out_shape=(pltpu.VMEM((2, 128, 256), F32), pltpu.VMEM((1024, 256), F32)),
        in_specs=[anywhere] * 6,
        out_specs=(pl.BlockSpec(memory_space=pltpu.VMEM), pl.BlockSpec(memory_space=pltpu.VMEM)),
        scratch_shapes=[
            pltpu.VMEM((2, NZ, 2, 2, 32, 1024), F32),
            pltpu.VMEM((2, 2, NZ, NY, 2, 48, 128), F32),
            pltpu.VMEM((2, 2, NZ, 32, 128), F32),
            pltpu.VMEM((2, 2, NY, 2, 128, 128), F32),
            pltpu.VMEM((2, 8, 256, 128), F32),
            pltpu.VMEM((4, 256, 256), F32),
            pltpu.VMEM((2, 128, 256), F32),
            pltpu.VMEM((1024, 256), F32),
            pltpu.SemaphoreType.DMA((N_SEND,)),
            pltpu.SemaphoreType.DMA((N_RECV,)),
            pltpu.SemaphoreType.DMA((11,)),
        ],
        compiler_params=pltpu.CompilerParams(
            collective_id=0, has_side_effects=True, vmem_limit_bytes=57 << 20),
    )(
        b_steps, b_trail, cross.T, jnp.swapaxes(trail, 1, 2),
        jnp.swapaxes(inv, 2, 3), jnp.swapaxes(low, 1, 2),
    )


def solution(mesh):
    placed = (
        P(None, "row", "col"),
        P("row", "col"),
        P("row", "col"),
        P(None, "row", "col"),
        P(None, None, None, "col"),
        P(None, None, "col"),
    )
    return jax.shard_map(
        shards,
        mesh=mesh,
        in_specs=placed,
        out_specs=(P(None, "row", "col"), P("row", "col")),
        check_vma=False,
    )
```

```python
import jax
import jax.numpy as jnp
from jax import lax
from jax.experimental import pallas as pl
from jax.experimental.pallas import tpu as pltpu
from jax.sharding import PartitionSpec as P

MESH = pl.DeviceIdType.MESH
F32 = jnp.float32
BF16 = jnp.bfloat16

NY, NZ = 4, 8
PAIRED = (-1,)
PAIRS = (0, 1, 3, 2)
N_SEND, N_RECV = 42, 128

ORDER = (
    ("tz",), ("first",), ("rs", 0), ("ring", 0, -1), ("load",), ("hop", 1, 0, -1), ("ring", 0, 1), ("tx", 0, 0),
    ("tx", 0, 3), ("tx", 0, 1), ("ro", 0, 0), ("tx", 0, 2), ("r0", 0), ("ro", 0, 1), ("ring", 1, 1), ("ring", 1, -1),
    ("tx", 1, 0), ("r1", 0, 0), ("ring", 2, 1), ("hop", 1, 0, 1), ("pair",), ("hop", 0, 0, -1), ("r1", 0, 1),
    ("ty", 0, 0), ("ring", 2, -1), ("ty", 0, 3), ("ring", 3, 1), ("tx", 1, 3), ("ty", 0, 1), ("hop", 0, 0, 1),
    ("ty", 0, 2), ("ty", 1, 0), ("tf", 0, 0, 1), ("hop", 1, 1, -1), ("tf", 0, 0, -1), ("hop", 1, 1, 1),
    ("ring", 4, 1), ("tf", 0, 3, 1), ("tf", 0, 3, -1), ("cross", 1, 0, 1), ("hop", 0, 1, -1), ("tf", 0, 1, 1),
    ("ring", 3, -1), ("cx",), ("tx", 1, 1), ("tf", 0, 1, -1), ("ty", 1, 3), ("tx", 1, 2), ("tf", 0, 2, 1),
    ("tf", 0, 2, -1), ("tf", 1, 0, 1), ("hop", 1, 2, -1), ("cross", 1, 1, 1), ("tf", 1, 0, -1), ("hop", 0, 1, 1),
    ("tk", 0, 0), ("tk", 0, 3), ("cross", 1, 1, -1), ("tk", 0, 1), ("hop", 1, 2, 1), ("ck",), ("tf", 1, 3, 1),
    ("ty", 1, 1), ("tf", 1, 3, -1), ("ty", 1, 2), ("tk", 0, 2), ("next",), ("rs", 1), ("tk", 1, 0), ("hop", 0, 2, 1),
    ("hop", 0, 2, -1), ("tk", 1, 3), ("cross", 1, 2, -1), ("tf", 1, 1, -1), ("tf", 1, 1, 1), ("tf", 1, 2, 1),
    ("tf", 1, 2, -1), ("trail", 0, 0), ("hop", 1, 3, -1), ("cross", 1, 2, 1), ("hop", 1, 3, 1), ("trail", 0, 1),
    ("ro", 1, 0), ("r0", 1), ("ro", 1, 1), ("tk", 1, 1), ("tk", 1, 2), ("hop", 0, 3, 1), ("hop", 0, 3, -1),
    ("r1", 1, 0), ("cross", 1, 3, -1), ("r1", 1, 1), ("trail", 0, 2), ("hop", 1, 4, -1), ("cross", 1, 3, 1),
    ("last",), ("trail", 1, 0), ("hop", 0, 4, 1), ("trail", 1, 1), ("early",), ("cross", 1, 4, -1), ("trail", 1, 2),
    ("trail", 0, 3), ("finish",),
)


def split(value):
    high = value.astype(BF16)
    return high, (value - high.astype(F32)).astype(BF16)


def product(left, right):
    dot = lambda a, b: jnp.dot(a, b, preferred_element_type=F32)
    return dot(left[0], right[0]) + (dot(left[0], right[1]) + dot(left[1], right[0]))


def kernel(
    b_steps, b_trail, cross, trail, inv, low,
    x_out, t_out,
    lf, tab, crs, rhs, xs, acc, bs, bt,
    ss, rs, ls,
):
    row, col = lax.axis_index("row"), lax.axis_index("col")
    xl, y = lax.div(row, NY), lax.rem(row, NY)
    z, xh, k = lax.div(col, 4), lax.rem(lax.div(col, 2), 2), lax.rem(col, 2)
    ys = [lax.rem(y + i, NY) for i in range(NY)]
    zs_at = [lax.rem(z + i, NZ) for i in range(NZ)]
    pairs = [lax.rem(lax.div(z, 2) + i, NZ // 2) for i in range(NZ // 2)]
    beside = z + 1 - 2 * lax.rem(z, 2)

    places_of = {}

    def dev(dxl=0, dy=0, dz=0, dxh=0, dk=0):
        return places_of[dxl, dy % NY, dz % NZ, dxh, dk]

    def greet(dxl=0, dy=0, dz=0, dxh=0, dk=0):
        at_row = ((1 - xl) if dxl else xl) * NY + ys[dy]
        at_col = zs_at[dz] * 4 + ((1 - xh) if dxh else xh) * 2 + ((1 - k) if dk else k)
        places_of[dxl, dy, dz, dxh, dk] = (at_row, at_col)
        return at_row, at_col

    ids, streams = {}, {}

    def sem(name):
        return ids.setdefault(name, len(ids))

    def out_sem(stream):
        return streams.setdefault(stream, len(streams))

    def send(stream, at, src, dst, to_dev, rs_name=None):
        pltpu.make_async_remote_copy(
            src_ref=src, dst_ref=dst, send_sem=ss.at[out_sem(stream)],
            recv_sem=rs.at[sem(rs_name or (stream if at is None else (stream, at)))],
            device_id=to_dev, device_id_type=MESH).start()

    def recv(stream, at, region, from_dev):
        i = sem(stream) if at is None else sem((stream, at)) if isinstance(at, tuple) else at
        pltpu.make_async_remote_copy(
            src_ref=region, dst_ref=region, send_sem=ss.at[out_sem(stream)], recv_sem=rs.at[i],
            device_id=from_dev, device_id_type=MESH).wait_recv()

    def sent(stream, region):
        pltpu.make_async_remote_copy(
            src_ref=region, dst_ref=region, send_sem=ss.at[streams[stream]], recv_sem=rs.at[0],
            device_id=dev(dk=1), device_id_type=MESH).wait_send()

    partners = [greet(dz=e) for e in range(1, NZ)] + [greet(dy=1), greet(dy=3), greet(dxl=1), greet(dxh=1), greet(dk=1)]
    barrier = pltpu.get_barrier_semaphore()
    for p in partners:
        pl.semaphore_signal(barrier, inc=1, device_id=p, device_id_type=MESH)
    loads = []

    def load(src, dst):
        copy = pltpu.make_async_copy(src, dst, ls.at[len(loads)])
        copy.start()
        loads.append(copy)

    lanes = pl.ds(pl.multiple_of(y * 128, 128), 128)
    load(b_steps, bs)
    load(cross, crs.at[k, xh, z])
    for s in range(2):
        mine = tab.at[s, k, z, y, xh]
        load(inv.at[s, 0, :, lanes], mine.at[pl.ds(0, 16)])
        load(low.at[s, :, lanes], mine.at[pl.ds(16, 16)])
        load(inv.at[s, 1, :, pl.ds(pl.multiple_of((NY - 1 - y) * 128, 128), 128)], mine.at[pl.ds(32, 16)])
    for s in range(2):
        load(trail.at[s], lf.at[s, z, k, xh])
    load(b_trail, bt)
    for c in loads[:8]:
        c.wait()
    pl.semaphore_wait(barrier, len(partners))

    def filled(zz, at_y, act):
        p, q = zz <= at_y, zz <= NY - 1 - at_y
        lax.cond(
            p,
            lambda: lax.cond(q, lambda: act(pl.ds(0, 48)), lambda: act(pl.ds(0, 32))),
            lambda: lax.cond(q, lambda: act(pl.ds(16, 32)), lambda: act(pl.ds(16, 16))),
        )

    def pair(d):
        return pairs[d]

    tz = [sem(("tz", e)) for e in range(NZ)]

    def t_zsend():
        def act(rows):
            blk = tab.at[0, k, z, y, xh, rows]
            for e in range(1, NZ):
                pltpu.make_async_remote_copy(
                    src_ref=blk, dst_ref=blk, send_sem=ss.at[out_sem("tz")], recv_sem=rs.at[tz[e]],
                    device_id=dev(dz=e), device_id_type=MESH).start()
        filled(pairs[0], y, act)

    def ring(h, sign):
        at = zrel(h if sign > 0 else NZ - h)
        last = h == (4 if sign > 0 else 3)
        blk = crs.at[k, xh, at]
        if h:
            recv("cr", (sign, h), blk, dev(dz=NZ - sign))
        if not last:
            send("cr", (sign, h + 1), blk, blk, dev(dz=sign % NZ))

        def act(rows):
            blk = tab.at[1, k, at, y, xh, rows]
            if h:
                recv(("tr", sign), (h,), blk, dev(dz=NZ - sign))
            if not last:
                send(("tr", sign, h), None, blk, blk, dev(dz=sign % NZ), rs_name=(("tr", sign), (h + 1,)))
        filled(lax.div(at, 2), y, act)

    def t_x(g, d):
        def act(rows):
            zz = pair(d)
            for from_z in () if g else (2 * zz, 2 * zz + 1) if d else (beside,):
                e = lax.rem(z - from_z + NZ, NZ)
                recv("tz", tz[0] + e, tab.at[g, k, from_z, y, xh, rows], dev(dz=1))
            blk = tab.at[g, k, pl.ds(2 * zz, 2), y, xh, rows]
            send(("tx", g), (d,), blk, blk, dev(dxh=1))
        filled(pair(d), y, act)

    def t_y(g, d):
        zs = pl.ds(2 * pair(d), 2)

        def act(rows):
            recv(("tx", g), (d,), tab.at[g, k, zs, y, 1 - xh, rows], dev(dxh=1))
            blk = tab.at[g, k, zs, y, :, rows]
            send(("ty+", g), (d,), blk, blk, dev(dy=1))
            send(("ty-", g), (d,), blk, blk, dev(dy=3))
        filled(pair(d), y, act)

    def t_f(g, d, sign):
        zs = pl.ds(2 * pair(d), 2)
        name, near, half = ("+", ys[3], 0) if sign > 0 else ("-", ys[1], 1)

        def act(rows):
            recv(("ty" + name, g), (d,), tab.at[g, k, zs, near, :, rows], dev(dy=NY - sign))
            blk = tab.at[g, k, zs, near, half, rows]
            send(("tf" + name, g), (d,), blk, blk, dev(dy=sign % NY))
        filled(pair(d), near, act)

    def t_k(g, d):
        zs = pl.ds(2 * pair(d), 2)
        far = ys[2]

        def act(rows):
            recv(("tf+", g), (d,), tab.at[g, k, zs, far, 0, rows], dev(dy=3))
            recv(("tf-", g), (d,), tab.at[g, k, zs, far, 1, rows], dev(dy=1))
        filled(pair(d), far, act)
        blk = tab.at[g, k, zs]
        send(("tk", g), None, blk, blk, dev(dk=1))

    def t_done(g):
        recv(("tk", g), None, tab.at[g, 1 - k], dev(dk=1))

    def t_sent(g):
        six = pl.ds(0, 6)
        if g == 0:
            filled(pairs[0], y, lambda rows: sent("tz", tab.at[g, k, pl.ds(0, NZ - 1), y, xh, rows]))
        else:
            for sign, last in ((1, 4), (-1, 3)):
                for h in range(last):
                    at = zrel(h if sign > 0 else NZ - h)
                    filled(lax.div(at, 2), y, lambda rows: sent(("tr", sign, h), tab.at[g, k, at, y, xh, rows]))
        sent(("tx", g), tab.at[g, k, six, y, xh])
        for sign in "+-":
            sent(("ty" + sign, g), tab.at[g, k, six, y])
            sent(("tf" + sign, g), tab.at[g, k, six, y, xh])
        sent(("tk", g), tab.at[g, k])

    def c_x():
        send("cx", None, crs.at[k, xh], crs.at[k, xh], dev(dxh=1))

    def c_k():
        recv("cx", None, crs.at[k, 1 - xh], dev(dxh=1))
        send("ck", None, crs.at[k], crs.at[k], dev(dk=1))

    def c_done():
        recv("ck", None, crs.at[1 - k], dev(dk=1))

    def c_sent():
        sent("cr", crs.at[k, xh, pl.ds(0, NZ - 1)])
        sent("cx", crs.at[k, xh])
        sent("ck", crs.at[k])

    def zrel(e):
        return zs_at[-e % NZ]

    def l_load():
        for c in loads[8:10]:
            c.wait()
        own = lf.at[0, z, k, xh]
        send("l0x", None, own, own, dev(dxh=1))

    def l_pair():
        recv("l0x", None, lf.at[0, z, k, 1 - xh], dev(dxh=1))

    def l_hop(s, h, sign):
        at = zrel(h if sign > 0 else NZ - h)
        blk = lf.at[s, at, k] if s == 0 else lf.at[s, at, k, xh]
        if h:
            recv(("l", s), (sign, h), blk, dev(dz=NZ - sign))
        if h < (4 if (s == 0) == (sign > 0) else 3):
            send(("l", s), (sign, h + 1), blk, blk, dev(dz=sign % NZ))
        if h == 0 and sign < 0:
            return
        if s == 0:
            send(("lk", s), (sign * h,), blk, blk, dev(dk=1))
        else:
            if not (h == 1 and sign in PAIRED):
                send(("lx", s), (sign * h,), blk, blk, dev(dxh=1))

    def l_cross(s, h, sign):
        at = zrel(h if sign > 0 else NZ - h)
        blk = lf.at[s, at, k, 1 - xh]
        if h == 1 and sign in PAIRED:
            recv("lp", (sign,), blk, dev(dz=NZ - sign))
        else:
            recv(("lx", s), (sign * h,), blk, dev(dxh=1))
        if h == 0:
            for side in PAIRED:
                send("lp", (side,), blk, blk, dev(dz=side % NZ))
        blk = lf.at[s, at, k]
        send(("lk", s), (sign * h,), blk, blk, dev(dk=1))

    def l_sent():
        sent("l0x", lf.at[0, z, k, xh])
        sent(("l", 0), lf.at[0, pl.ds(0, NZ - 1), k])
        sent(("l", 1), lf.at[1, pl.ds(0, NZ - 1), k, xh])
        sent(("lx", 1), lf.at[1, pl.ds(0, NZ - len(PAIRED)), k, xh])
        if PAIRED:
            sent("lp", lf.at[1, pl.ds(0, len(PAIRED)), k, xh])
        for s in range(2):
            sent(("lk", s), lf.at[s, :, k])

    def r_send(g):
        for h in range(2):
            blk = rhs.at[g, xl, y, h]
            send(("rx", g), (h,), blk, blk, dev(dxl=1))
        blk = rhs.at[g, xl, y]
        send(("ry", g), ("+",), blk, blk, dev(dy=1))
        send(("ry", g), ("-",), blk, blk, dev(dy=3))

    def r_other(g, h):
        blk = rhs.at[g, 1 - xl, y, h]
        recv(("rx", g), (h,), blk, dev(dxl=1))
        send(("ro", g), ("+", h), blk, blk, dev(dy=1))
        send(("ro", g), ("-", h), blk, blk, dev(dy=3))

    def r_f0(g):
        blk = rhs.at[g, xl, ys[3]]
        recv(("ry", g), ("+",), blk, dev(dy=3))
        send(("rf", g), None, blk, blk, dev(dy=1))

    def r_f1(g, h):
        blk = rhs.at[g, 1 - xl, ys[1], h]
        recv(("ro", g), ("-", h), blk, dev(dy=1))
        send(("rg", g), (h,), blk, blk, dev(dy=3))

    def r_done(g):
        far = ys[2]
        recv(("ry", g), ("-",), rhs.at[g, xl, ys[1]], dev(dy=1))
        recv(("rf", g), None, rhs.at[g, xl, far], dev(dy=3))
        for h in range(2):
            recv(("ro", g), ("+", h), rhs.at[g, 1 - xl, ys[3], h], dev(dy=3))
            recv(("rg", g), (h,), rhs.at[g, 1 - xl, far, h], dev(dy=1))

    def r_sent(g):
        sent(("rx", g), rhs.at[g, xl, y])
        sent(("ry", g), rhs.at[g, xl, pl.ds(0, 2)])
        sent(("ro", g), rhs.at[g, xl, pl.ds(0, 2)])
        sent(("rf", g), rhs.at[g, xl, y])
        sent(("rg", g), rhs.at[g, xl, y])

    places = [(a, c, b) for a in range(NZ) for b in range(2) for c in range(2)]

    def weights(s, which, two):
        deep = NZ if which == 1 else 4 * two + 4
        halves = []
        for m in (2 * two, 2 * two + 1):
            at = NY - 1 - m if which == 2 else m
            halves.append(jnp.concatenate([
                tab[s, c, a, at, b, 16 * which:16 * which + 16, :] if which == 1 or a // 2 <= m
                else jnp.zeros((16, 128), F32)
                for a, c, b in places if a < deep], axis=0))
        return split(jnp.concatenate(halves, axis=1))

    def part(pair_of, two):
        return tuple(v[:, :256 * two + 256] for v in pair_of)

    def blocks(g, x):
        return [rhs[g, x, j].reshape(256, 128) for j in range(NY)]

    def solve(s):
        top = split(jnp.concatenate(blocks(s, 0), axis=1))
        out = [product(part(top, two), weights(s, 0, two)) for two in range(2)]
        for j in range(4):
            xs[s, j] = out[j // 2][:, 128 * (j % 2):128 * (j % 2) + 128]
        first = split(jnp.concatenate(out, axis=1))
        out = [product(first, weights(s, 1, two)) for two in range(2)]
        rest = split(jnp.concatenate(blocks(s, 1), axis=1) - jnp.concatenate(out, axis=1))
        out = [product(part(rest, two), weights(s, 2, two)) for two in range(2)]
        for j in range(4):
            xs[s, 4 + j] = out[j // 2][:, 128 * (j % 2):128 * (j % 2) + 128]

    def whole(s):
        return split(jnp.concatenate([xs[s, j] for j in range(8)], axis=1))

    def emit(s):
        x_out[s] = xs[s, row].T

    def r_first():
        rhs[0, xl, y] = bs[0].T.reshape(2, 128, 128)

    def r_next():
        r_done(0)
        t_done(0)
        c_done()
        solve(0)
        low_cross = split(jnp.concatenate([crs[c, b, a] for a, c, b in places], axis=0))
        rhs[1, xl, y] = (bs[1].T - product(whole(0), low_cross)).reshape(2, 128, 128)

    def trail_part(s, i):
        ats = []
        for h in (-i, i + 1) if s == 0 else (i, -i - 1):
            at = zrel(h if h >= 0 else NZ + h)
            recv(("lk", s), (h,), lf.at[s, at, 1 - k], dev(dk=1))
            ats.append(at)
        return split(jnp.concatenate([xs[s, at] for at in ats], axis=1)), ats

    def right(s, ats, lane):
        return split(jnp.concatenate([lf[s, at, c, b, :, lane] for at in ats for b in range(2) for c in range(2)], axis=0))

    def trail(s, i):
        left, ats = trail_part(s, i)

        @pl.loop(0, 4)
        def _(j):
            out = product(left, right(s, ats, pl.ds(pl.multiple_of(j * 256, 256), 256)))
            acc[j] = out if s == 0 and i == 0 else acc[j] + out

    def solve_last():
        emit(0)
        r_done(1)
        t_done(1)
        solve(1)
        emit(1)
        loads[10].wait()

    def early():
        t_sent(0)
        r_sent(0)
        c_sent()
        t_sent(1)

    def finish():
        r_sent(1)
        left, ats = trail_part(1, 3)
        for j in range(4):
            at = slice(256 * j, 256 * j + 256)
            t_out[at, :] = bt[at, :] - (acc[j] + product(left, right(1, ats, at))).T

    for step, *at in ORDER:
        {
            "tz": t_zsend, "ring": ring, "tx": t_x, "ty": t_y, "tf": t_f, "tk": t_k, "cx": c_x, "ck": c_k,
            "load": l_load, "pair": l_pair, "hop": l_hop, "cross": l_cross, "rs": r_send, "ro": r_other, "r0": r_f0, "r1": r_f1,
            "first": r_first, "next": r_next, "trail": trail, "last": solve_last, "early": early, "finish": finish,
        }[step](*at)
    l_sent()
    assert len(ids) <= N_RECV and len(streams) <= N_SEND, (len(ids), len(streams))


def shards(b_steps, b_trail, cross, trail, inv, low):
    anywhere = pl.BlockSpec(memory_space=pl.ANY)
    return pl.pallas_call(
        kernel,
        out_shape=(pltpu.VMEM((2, 128, 256), F32), pltpu.VMEM((1024, 256), F32)),
        in_specs=[anywhere] * 6,
        out_specs=(pl.BlockSpec(memory_space=pltpu.VMEM), pl.BlockSpec(memory_space=pltpu.VMEM)),
        scratch_shapes=[
            pltpu.VMEM((2, NZ, 2, 2, 32, 1024), F32),
            pltpu.VMEM((2, 2, NZ, NY, 2, 48, 128), F32),
            pltpu.VMEM((2, 2, NZ, 32, 128), F32),
            pltpu.VMEM((2, 2, NY, 2, 128, 128), F32),
            pltpu.VMEM((2, 8, 256, 128), F32),
            pltpu.VMEM((4, 256, 256), F32),
            pltpu.VMEM((2, 128, 256), F32),
            pltpu.VMEM((1024, 256), F32),
            pltpu.SemaphoreType.DMA((N_SEND,)),
            pltpu.SemaphoreType.DMA((N_RECV,)),
            pltpu.SemaphoreType.DMA((11,)),
        ],
        compiler_params=pltpu.CompilerParams(
            collective_id=0, has_side_effects=True, vmem_limit_bytes=57 << 20),
    )(
        b_steps, b_trail, cross.T, jnp.swapaxes(trail, 1, 2),
        jnp.swapaxes(inv, 2, 3), jnp.swapaxes(low, 1, 2),
    )


def solution(mesh):
    placed = (
        P(None, "row", "col"),
        P("row", "col"),
        P("row", "col"),
        P(None, "row", "col"),
        P(None, None, None, "col"),
        P(None, None, "col"),
    )
    return jax.shard_map(
        shards,
        mesh=mesh,
        in_specs=placed,
        out_specs=(P(None, "row", "col"), P("row", "col")),
        check_vma=False,
    )
```

```python
import jax
import jax.numpy as jnp
from jax import lax
from jax.experimental import pallas as pl
from jax.experimental.pallas import tpu as pltpu
from jax.sharding import PartitionSpec as P

MESH = pl.DeviceIdType.MESH
F32 = jnp.float32
BF16 = jnp.bfloat16

NY, NZ = 4, 8
PAIRED = (-1,)
PAIRS = (0, 1, 3, 2)
N_SEND, N_RECV = 42, 128

ORDER = (
    ("tz",), ("first",), ("rs", 0), ("ring", 0, -1), ("load",), ("hop", 1, 0, -1), ("ring", 0, 1), ("tx", 0, 0),
    ("tx", 0, 3), ("tx", 0, 1), ("ro", 0, 0), ("tx", 0, 2), ("r0", 0), ("ro", 0, 1), ("ring", 1, 1), ("ring", 1, -1),
    ("tx", 1, 0), ("r1", 0, 0), ("ring", 2, 1), ("hop", 1, 0, 1), ("pair",), ("hop", 0, 0, -1), ("r1", 0, 1),
    ("ty", 0, 0), ("ring", 2, -1), ("ty", 0, 3), ("ring", 3, 1), ("tx", 1, 3), ("ty", 0, 1), ("hop", 0, 0, 1),
    ("ty", 0, 2), ("ty", 1, 0), ("tf", 0, 0, 1), ("hop", 1, 1, -1), ("tf", 0, 0, -1), ("hop", 1, 1, 1),
    ("ring", 4, 1), ("tf", 0, 3, 1), ("tf", 0, 3, -1), ("cross", 1, 0, 1), ("hop", 0, 1, -1), ("tf", 0, 1, 1),
    ("ring", 3, -1), ("cx",), ("tx", 1, 1), ("tf", 0, 1, -1), ("ty", 1, 3), ("tx", 1, 2), ("tf", 0, 2, 1),
    ("tf", 0, 2, -1), ("tf", 1, 0, 1), ("hop", 1, 2, -1), ("cross", 1, 1, 1), ("tf", 1, 0, -1), ("hop", 0, 1, 1),
    ("tk", 0, 0), ("tk", 0, 3), ("cross", 1, 1, -1), ("tk", 0, 1), ("hop", 1, 2, 1), ("ck",), ("tf", 1, 3, 1),
    ("ty", 1, 1), ("tf", 1, 3, -1), ("ty", 1, 2), ("tk", 0, 2), ("next",), ("rs", 1), ("tk", 1, 0), ("hop", 0, 2, 1),
    ("hop", 0, 2, -1), ("tk", 1, 3), ("cross", 1, 2, -1), ("tf", 1, 1, -1), ("tf", 1, 1, 1), ("tf", 1, 2, 1),
    ("tf", 1, 2, -1), ("trail", 0, 0), ("hop", 1, 3, -1), ("cross", 1, 2, 1), ("hop", 1, 3, 1), ("trail", 0, 1),
    ("ro", 1, 0), ("r0", 1), ("ro", 1, 1), ("tk", 1, 1), ("tk", 1, 2), ("hop", 0, 3, 1), ("hop", 0, 3, -1),
    ("r1", 1, 0), ("cross", 1, 3, -1), ("r1", 1, 1), ("trail", 0, 2), ("hop", 1, 4, -1), ("cross", 1, 3, 1),
    ("last",), ("trail", 1, 0), ("hop", 0, 4, 1), ("trail", 1, 1), ("early",), ("cross", 1, 4, -1), ("trail", 1, 2),
    ("trail", 0, 3), ("finish",),
)


def split(value):
    high = value.astype(BF16)
    return high, (value - high.astype(F32)).astype(BF16)


def product(left, right):
    dot = lambda a, b: jnp.dot(a, b, preferred_element_type=F32)
    return dot(left[0], right[0]) + (dot(left[0], right[1]) + dot(left[1], right[0]))


def kernel(
    b_steps, b_trail, cross, trail, inv, low,
    x_out, t_out,
    lf, tab, crs, rhs, xs, acc, bs, bt,
    ss, rs, ls,
):
    row, col = lax.axis_index("row"), lax.axis_index("col")
    xl, y = lax.div(row, NY), lax.rem(row, NY)
    z, xh, k = lax.div(col, 4), lax.rem(lax.div(col, 2), 2), lax.rem(col, 2)
    ys = [lax.rem(y + i, NY) for i in range(NY)]
    zs_at = [lax.rem(z + i, NZ) for i in range(NZ)]
    pairs = [lax.rem(lax.div(z, 2) + i, NZ // 2) for i in range(NZ // 2)]
    beside = z + 1 - 2 * lax.rem(z, 2)

    places_of = {}

    def dev(dxl=0, dy=0, dz=0, dxh=0, dk=0):
        return places_of[dxl, dy % NY, dz % NZ, dxh, dk]

    def greet(dxl=0, dy=0, dz=0, dxh=0, dk=0):
        at_row = ((1 - xl) if dxl else xl) * NY + ys[dy]
        at_col = zs_at[dz] * 4 + ((1 - xh) if dxh else xh) * 2 + ((1 - k) if dk else k)
        places_of[dxl, dy, dz, dxh, dk] = (at_row, at_col)
        return at_row, at_col

    ids, streams = {}, {}

    def sem(name):
        return ids.setdefault(name, len(ids))

    def out_sem(stream):
        return streams.setdefault(stream, len(streams))

    def send(stream, at, src, dst, to_dev, rs_name=None):
        pltpu.make_async_remote_copy(
            src_ref=src, dst_ref=dst, send_sem=ss.at[out_sem(stream)],
            recv_sem=rs.at[sem(rs_name or (stream if at is None else (stream, at)))],
            device_id=to_dev, device_id_type=MESH).start()

    def recv(stream, at, region, from_dev):
        i = sem(stream) if at is None else sem((stream, at)) if isinstance(at, tuple) else at
        pltpu.make_async_remote_copy(
            src_ref=region, dst_ref=region, send_sem=ss.at[out_sem(stream)], recv_sem=rs.at[i],
            device_id=from_dev, device_id_type=MESH).wait_recv()

    def sent(stream, region):
        pltpu.make_async_remote_copy(
            src_ref=region, dst_ref=region, send_sem=ss.at[streams[stream]], recv_sem=rs.at[0],
            device_id=dev(dk=1), device_id_type=MESH).wait_send()

    partners = [greet(dz=e) for e in range(1, NZ)] + [greet(dy=1), greet(dy=3), greet(dxl=1), greet(dxh=1), greet(dk=1)]
    barrier = pltpu.get_barrier_semaphore()
    for p in partners:
        pl.semaphore_signal(barrier, inc=1, device_id=p, device_id_type=MESH)
    loads = []

    def load(src, dst):
        copy = pltpu.make_async_copy(src, dst, ls.at[len(loads)])
        copy.start()
        loads.append(copy)

    lanes = pl.ds(pl.multiple_of(y * 128, 128), 128)
    load(b_steps, bs)
    load(cross, crs.at[k, xh, z])
    for s in range(2):
        mine = tab.at[s, k, z, y, xh]
        load(inv.at[s, 0, :, lanes], mine.at[pl.ds(0, 16)])
        load(low.at[s, :, lanes], mine.at[pl.ds(16, 16)])
        load(inv.at[s, 1, :, pl.ds(pl.multiple_of((NY - 1 - y) * 128, 128), 128)], mine.at[pl.ds(32, 16)])
    for s in range(2):
        load(trail.at[s], lf.at[s, z, k, xh])
    load(b_trail, bt)
    for c in loads[:8]:
        c.wait()
    pl.semaphore_wait(barrier, len(partners))

    def filled(zz, at_y, act):
        p, q = zz <= at_y, zz <= NY - 1 - at_y
        lax.cond(
            p,
            lambda: lax.cond(q, lambda: act(pl.ds(0, 48)), lambda: act(pl.ds(0, 32))),
            lambda: lax.cond(q, lambda: act(pl.ds(16, 32)), lambda: act(pl.ds(16, 16))),
        )

    def pair(d):
        return pairs[d]

    tz = [sem(("tz", e)) for e in range(NZ)]

    def t_zsend():
        def act(rows):
            blk = tab.at[0, k, z, y, xh, rows]
            for e in range(1, NZ):
                pltpu.make_async_remote_copy(
                    src_ref=blk, dst_ref=blk, send_sem=ss.at[out_sem("tz")], recv_sem=rs.at[tz[e]],
                    device_id=dev(dz=e), device_id_type=MESH).start()
        filled(pairs[0], y, act)

    def ring(h, sign):
        at = zrel(h if sign > 0 else NZ - h)
        last = h == (4 if sign > 0 else 3)
        blk = crs.at[k, xh, at]
        if h:
            recv("cr", (sign, h), blk, dev(dz=NZ - sign))
        if not last:
            send("cr", (sign, h + 1), blk, blk, dev(dz=sign % NZ))

        def act(rows):
            blk = tab.at[1, k, at, y, xh, rows]
            if h:
                recv(("tr", sign), (h,), blk, dev(dz=NZ - sign))
            if not last:
                send(("tr", sign, h), None, blk, blk, dev(dz=sign % NZ), rs_name=(("tr", sign), (h + 1,)))
        filled(lax.div(at, 2), y, act)

    def t_x(g, d):
        def act(rows):
            zz = pair(d)
            for from_z in () if g else (2 * zz, 2 * zz + 1) if d else (beside,):
                e = lax.rem(z - from_z + NZ, NZ)
                recv("tz", tz[0] + e, tab.at[g, k, from_z, y, xh, rows], dev(dz=1))
            blk = tab.at[g, k, pl.ds(2 * zz, 2), y, xh, rows]
            send(("tx", g), (d,), blk, blk, dev(dxh=1))
        filled(pair(d), y, act)

    def t_y(g, d):
        zs = pl.ds(2 * pair(d), 2)

        def act(rows):
            recv(("tx", g), (d,), tab.at[g, k, zs, y, 1 - xh, rows], dev(dxh=1))
            blk = tab.at[g, k, zs, y, :, rows]
            send(("ty+", g), (d,), blk, blk, dev(dy=1))
            send(("ty-", g), (d,), blk, blk, dev(dy=3))
        filled(pair(d), y, act)

    def t_f(g, d, sign):
        zs = pl.ds(2 * pair(d), 2)
        name, near, half = ("+", ys[3], 0) if sign > 0 else ("-", ys[1], 1)

        def act(rows):
            recv(("ty" + name, g), (d,), tab.at[g, k, zs, near, :, rows], dev(dy=NY - sign))
            blk = tab.at[g, k, zs, near, half, rows]
            send(("tf" + name, g), (d,), blk, blk, dev(dy=sign % NY))
        filled(pair(d), near, act)

    def t_k(g, d):
        zs = pl.ds(2 * pair(d), 2)
        far = ys[2]

        def act(rows):
            recv(("tf+", g), (d,), tab.at[g, k, zs, far, 0, rows], dev(dy=3))
            recv(("tf-", g), (d,), tab.at[g, k, zs, far, 1, rows], dev(dy=1))
        filled(pair(d), far, act)
        blk = tab.at[g, k, zs]
        send(("tk", g), None, blk, blk, dev(dk=1))

    def t_done(g):
        recv(("tk", g), None, tab.at[g, 1 - k], dev(dk=1))

    def t_sent(g):
        six = pl.ds(0, 6)
        if g == 0:
            filled(pairs[0], y, lambda rows: sent("tz", tab.at[g, k, pl.ds(0, NZ - 1), y, xh, rows]))
        else:
            for sign, last in ((1, 4), (-1, 3)):
                for h in range(last):
                    at = zrel(h if sign > 0 else NZ - h)
                    filled(lax.div(at, 2), y, lambda rows: sent(("tr", sign, h), tab.at[g, k, at, y, xh, rows]))
        sent(("tx", g), tab.at[g, k, six, y, xh])
        for sign in "+-":
            sent(("ty" + sign, g), tab.at[g, k, six, y])
            sent(("tf" + sign, g), tab.at[g, k, six, y, xh])
        sent(("tk", g), tab.at[g, k])

    def c_x():
        send("cx", None, crs.at[k, xh], crs.at[k, xh], dev(dxh=1))

    def c_k():
        recv("cx", None, crs.at[k, 1 - xh], dev(dxh=1))
        send("ck", None, crs.at[k], crs.at[k], dev(dk=1))

    def c_done():
        recv("ck", None, crs.at[1 - k], dev(dk=1))

    def c_sent():
        sent("cr", crs.at[k, xh, pl.ds(0, NZ - 1)])
        sent("cx", crs.at[k, xh])
        sent("ck", crs.at[k])

    def zrel(e):
        return zs_at[-e % NZ]

    def l_load():
        for c in loads[8:10]:
            c.wait()
        own = lf.at[0, z, k, xh]
        send("l0x", None, own, own, dev(dxh=1))

    def l_pair():
        recv("l0x", None, lf.at[0, z, k, 1 - xh], dev(dxh=1))

    def l_hop(s, h, sign):
        at = zrel(h if sign > 0 else NZ - h)
        blk = lf.at[s, at, k] if s == 0 else lf.at[s, at, k, xh]
        if h:
            recv(("l", s), (sign, h), blk, dev(dz=NZ - sign))
        if h < (4 if (s == 0) == (sign > 0) else 3):
            send(("l", s), (sign, h + 1), blk, blk, dev(dz=sign % NZ))
        if h == 0 and sign < 0:
            return
        if s == 0:
            send(("lk", s), (sign * h,), blk, blk, dev(dk=1))
        else:
            if not (h == 1 and sign in PAIRED):
                send(("lx", s), (sign * h,), blk, blk, dev(dxh=1))

    def l_cross(s, h, sign):
        at = zrel(h if sign > 0 else NZ - h)
        blk = lf.at[s, at, k, 1 - xh]
        if h == 1 and sign in PAIRED:
            recv("lp", (sign,), blk, dev(dz=NZ - sign))
        else:
            recv(("lx", s), (sign * h,), blk, dev(dxh=1))
        if h == 0:
            for side in PAIRED:
                send("lp", (side,), blk, blk, dev(dz=side % NZ))
        blk = lf.at[s, at, k]
        send(("lk", s), (sign * h,), blk, blk, dev(dk=1))

    def l_sent():
        sent("l0x", lf.at[0, z, k, xh])
        sent(("l", 0), lf.at[0, pl.ds(0, NZ - 1), k])
        sent(("l", 1), lf.at[1, pl.ds(0, NZ - 1), k, xh])
        sent(("lx", 1), lf.at[1, pl.ds(0, NZ - len(PAIRED)), k, xh])
        if PAIRED:
            sent("lp", lf.at[1, pl.ds(0, len(PAIRED)), k, xh])
        for s in range(2):
            sent(("lk", s), lf.at[s, :, k])

    def r_send(g):
        for h in range(2):
            blk = rhs.at[g, xl, y, h]
            send(("rx", g), (h,), blk, blk, dev(dxl=1))
        blk = rhs.at[g, xl, y]
        send(("ry", g), ("+",), blk, blk, dev(dy=1))
        send(("ry", g), ("-",), blk, blk, dev(dy=3))

    def r_other(g, h):
        blk = rhs.at[g, 1 - xl, y, h]
        recv(("rx", g), (h,), blk, dev(dxl=1))
        send(("ro", g), ("+", h), blk, blk, dev(dy=1))
        send(("ro", g), ("-", h), blk, blk, dev(dy=3))

    def r_f0(g):
        blk = rhs.at[g, xl, ys[3]]
        recv(("ry", g), ("+",), blk, dev(dy=3))
        send(("rf", g), None, blk, blk, dev(dy=1))

    def r_f1(g, h):
        blk = rhs.at[g, 1 - xl, ys[1], h]
        recv(("ro", g), ("-", h), blk, dev(dy=1))
        send(("rg", g), (h,), blk, blk, dev(dy=3))

    def r_done(g):
        far = ys[2]
        recv(("ry", g), ("-",), rhs.at[g, xl, ys[1]], dev(dy=1))
        recv(("rf", g), None, rhs.at[g, xl, far], dev(dy=3))
        for h in range(2):
            recv(("ro", g), ("+", h), rhs.at[g, 1 - xl, ys[3], h], dev(dy=3))
            recv(("rg", g), (h,), rhs.at[g, 1 - xl, far, h], dev(dy=1))

    def r_sent(g):
        sent(("rx", g), rhs.at[g, xl, y])
        sent(("ry", g), rhs.at[g, xl, pl.ds(0, 2)])
        sent(("ro", g), rhs.at[g, xl, pl.ds(0, 2)])
        sent(("rf", g), rhs.at[g, xl, y])
        sent(("rg", g), rhs.at[g, xl, y])

    places = [(a, c, b) for a in range(NZ) for b in range(2) for c in range(2)]

    def weights(s, which, two):
        deep = NZ if which == 1 else 4 * two + 4
        halves = []
        for m in (2 * two, 2 * two + 1):
            at = NY - 1 - m if which == 2 else m
            halves.append(jnp.concatenate([
                tab[s, c, a, at, b, 16 * which:16 * which + 16, :] if which == 1 or a // 2 <= m
                else jnp.zeros((16, 128), F32)
                for a, c, b in places if a < deep], axis=0))
        return split(jnp.concatenate(halves, axis=1))

    def part(pair_of, two):
        return tuple(v[:, :256 * two + 256] for v in pair_of)

    def blocks(g, x):
        return [rhs[g, x, j].reshape(256, 128) for j in range(NY)]

    def solve(s):
        top = split(jnp.concatenate(blocks(s, 0), axis=1))
        out = [product(part(top, two), weights(s, 0, two)) for two in range(2)]
        for j in range(4):
            xs[s, j] = out[j // 2][:, 128 * (j % 2):128 * (j % 2) + 128]
        first = split(jnp.concatenate(out, axis=1))
        out = [product(first, weights(s, 1, two)) for two in range(2)]
        rest = split(jnp.concatenate(blocks(s, 1), axis=1) - jnp.concatenate(out, axis=1))
        out = [product(part(rest, two), weights(s, 2, two)) for two in range(2)]
        for j in range(4):
            xs[s, 4 + j] = out[j // 2][:, 128 * (j % 2):128 * (j % 2) + 128]

    def whole(s):
        return split(jnp.concatenate([xs[s, j] for j in range(8)], axis=1))

    def emit(s):
        x_out[s] = xs[s, row].T

    def r_first():
        rhs[0, xl, y] = bs[0].T.reshape(2, 128, 128)

    def r_next():
        r_done(0)
        t_done(0)
        c_done()
        solve(0)
        low_cross = split(jnp.concatenate([crs[c, b, a] for a, c, b in places], axis=0))
        rhs[1, xl, y] = (bs[1].T - product(whole(0), low_cross)).reshape(2, 128, 128)

    def trail_part(s, i):
        ats = []
        for h in (-i, i + 1) if s == 0 else (i, -i - 1):
            at = zrel(h if h >= 0 else NZ + h)
            recv(("lk", s), (h,), lf.at[s, at, 1 - k], dev(dk=1))
            ats.append(at)
        return split(jnp.concatenate([xs[s, at] for at in ats], axis=1)), ats

    def right(s, ats, lane):
        return split(jnp.concatenate([lf[s, at, c, b, :, lane] for at in ats for b in range(2) for c in range(2)], axis=0))

    def trail(s, i):
        left, ats = trail_part(s, i)

        @pl.loop(0, 4)
        def _(j):
            out = product(left, right(s, ats, pl.ds(pl.multiple_of(j * 256, 256), 256)))
            acc[j] = out if s == 0 and i == 0 else acc[j] + out

    def solve_last():
        emit(0)
        r_done(1)
        t_done(1)
        solve(1)
        emit(1)
        loads[10].wait()

    def early():
        t_sent(0)
        r_sent(0)
        c_sent()
        t_sent(1)

    def finish():
        r_sent(1)
        l_sent()
        left, ats = trail_part(1, 3)
        for j in range(4):
            at = slice(256 * j, 256 * j + 256)
            t_out[at, :] = bt[at, :] - (acc[j] + product(left, right(1, ats, at))).T

    for step, *at in ORDER:
        {
            "tz": t_zsend, "ring": ring, "tx": t_x, "ty": t_y, "tf": t_f, "tk": t_k, "cx": c_x, "ck": c_k,
            "load": l_load, "pair": l_pair, "hop": l_hop, "cross": l_cross, "rs": r_send, "ro": r_other, "r0": r_f0, "r1": r_f1,
            "first": r_first, "next": r_next, "trail": trail, "last": solve_last, "early": early, "finish": finish,
        }[step](*at)
    assert len(ids) <= N_RECV and len(streams) <= N_SEND, (len(ids), len(streams))


def shards(b_steps, b_trail, cross, trail, inv, low):
    anywhere = pl.BlockSpec(memory_space=pl.ANY)
    return pl.pallas_call(
        kernel,
        out_shape=(pltpu.VMEM((2, 128, 256), F32), pltpu.VMEM((1024, 256), F32)),
        in_specs=[anywhere] * 6,
        out_specs=(pl.BlockSpec(memory_space=pltpu.VMEM), pl.BlockSpec(memory_space=pltpu.VMEM)),
        scratch_shapes=[
            pltpu.VMEM((2, NZ, 2, 2, 32, 1024), F32),
            pltpu.VMEM((2, 2, NZ, NY, 2, 48, 128), F32),
            pltpu.VMEM((2, 2, NZ, 32, 128), F32),
            pltpu.VMEM((2, 2, NY, 2, 128, 128), F32),
            pltpu.VMEM((2, 8, 256, 128), F32),
            pltpu.VMEM((4, 256, 256), F32),
            pltpu.VMEM((2, 128, 256), F32),
            pltpu.VMEM((1024, 256), F32),
            pltpu.SemaphoreType.DMA((N_SEND,)),
            pltpu.SemaphoreType.DMA((N_RECV,)),
            pltpu.SemaphoreType.DMA((11,)),
        ],
        compiler_params=pltpu.CompilerParams(
            collective_id=0, has_side_effects=True, vmem_limit_bytes=57 << 20),
    )(
        b_steps, b_trail, cross.T, jnp.swapaxes(trail, 1, 2),
        jnp.swapaxes(inv, 2, 3), jnp.swapaxes(low, 1, 2),
    )


def solution(mesh):
    placed = (
        P(None, "row", "col"),
        P("row", "col"),
        P("row", "col"),
        P(None, "row", "col"),
        P(None, None, None, "col"),
        P(None, None, "col"),
    )
    return jax.shard_map(
        shards,
        mesh=mesh,
        in_specs=placed,
        out_specs=(P(None, "row", "col"), P("row", "col")),
        check_vma=False,
    )
```
